256 devices in a mesh: dp: 8 (over y, core), fsdp: 32 (over x, z).
Axes of the slice: x: 4, y: 4, z: 8, core: 2. Of those that a mesh axis runs over, the one named last changes fastest.
Arguments:
- acts: bfloat16 [32768, 8192], P(('dp', 'fsdp')), may hold values from -3 to 3
- out_grads: bfloat16 [32768, 8192], P(('dp', 'fsdp')), may hold values from -6 to 6
- token_counts: int32 [8], replicated, may hold values from 2048 to 4096, as said below
- k_factor: float32 [32, 256, 512], P('fsdp'), may hold values from -0.1875 to 2.44
- c_factor: float32 [32, 256, 512], P('fsdp'), may hold values from -0.1875 to 2.44
- k_moment: float32 [32, 256, 512], P('fsdp'), may hold values from -0.046875 to 0.946875
- c_moment: float32 [32, 256, 512], P('fsdp'), may hold values from -0.046875 to 0.946875
- grad_weight: bfloat16 [8192, 8192], P('dp', 'fsdp'), may hold values from -6 to 6
Outputs:
- k_factor_new: float32 [32, 256, 512], P('fsdp')
- c_factor_new: float32 [32, 256, 512], P('fsdp')
- k_moment_new: float32 [32, 256, 512], P('fsdp')
- c_moment_new: float32 [32, 256, 512], P('fsdp')
- precond: bfloat16 [8192, 8192], P('dp', 'fsdp')
The draws below stay inside these ranges and needn't reach their ends.
Inputs may be any that keep to these rules, and one draw needn't show every extreme that they name: `token_counts`: some data group has all 4096 slots valid and some other has exactly 2048.
All inputs are finite; a program needn't handle non-finite values.
Results may differ from the reference program's by a relative error of at most 0.0081.
Values may be sent and summed in bfloat16 or wider, within the bound.
A program may use at most 64 MiB of HBM per device.

```python
import math
import jax
import jax.numpy as jnp
from jax import lax

D = 8192
BS = 256
NB = 32
GROUP_TOK = 4096
TOKENS = 32768
N_DP = 8


def clipped_normal(key, shape):
    return jnp.clip(jax.random.normal(key, shape, jnp.float32), -4.0, 4.0)


def factor_draw(key):
    keys = jax.random.split(key, 4)
    shape = (NB, BS, BS)
    noise = clipped_normal(keys[0], shape)
    side = clipped_normal(keys[1], shape)
    scales = jnp.exp(jax.random.uniform(keys[2], (NB, 1, 1), jnp.float32, math.log(0.5), math.log(1.5)))
    rough = jnp.exp(jax.random.uniform(keys[3], (NB, 1, BS), jnp.float32, math.log(0.6), math.log(1.4)))
    identity = jnp.eye(BS, dtype=jnp.float32)
    blocks = scales * (identity * rough + noise * (0.5 / math.sqrt(BS)))
    border = side * (0.35 / math.sqrt(BS))
    return jnp.concatenate([blocks, border], axis=-1)


def moment_draw(key):
    keys = jax.random.split(key, 3)
    shape = (NB, BS, BS)
    noise = clipped_normal(keys[0], shape)
    side = clipped_normal(keys[1], shape)
    level = jax.random.uniform(keys[2], (NB, 1, BS), jnp.float32, 0.1, 0.9)
    identity = jnp.eye(BS, dtype=jnp.float32)
    blocks = identity * level + noise * (3.0 / BS)
    border = side * (2.0 / BS)
    return jnp.concatenate([blocks, border], axis=-1)


def draw_token_counts(key, part):
    keys = jax.random.split(jax.random.fold_in(key, 71), 2)
    counts = jax.random.randint(keys[0], (N_DP,), GROUP_TOK // 2, GROUP_TOK + 1)
    order = jax.random.permutation(keys[1], N_DP)
    counts = jnp.where(order == 0, GROUP_TOK, counts)
    counts = jnp.where(order == 1, GROUP_TOK // 2, counts)
    return counts.astype(jnp.int32)


def draw_k_factor(key, part):
    return factor_draw(jax.random.fold_in(key, 17))


def draw_c_factor(key, part):
    return factor_draw(jax.random.fold_in(key, 29))


def draw_k_moment(key, part):
    return moment_draw(jax.random.fold_in(key, 41))


def draw_c_moment(key, part):
    return moment_draw(jax.random.fold_in(key, 53))


def level_of(key, extent, cuts, low, top_value):
    gain, own = 1.0, jax.random.fold_in(key, 6)
    for axis_at, shards_of in cuts:
        steps = jnp.exp(jax.random.uniform(jax.random.fold_in(own, axis_at), (shards_of,), jnp.float32, low / len(cuts), top_value / len(cuts)))
        gain = gain * jnp.repeat(steps, extent[axis_at] // shards_of).reshape([-1 if axis == axis_at else 1 for axis in range(len(extent))])
    return gain


def gaussian(rng, dims, deviation, limit, cuts=(), kind=jnp.bfloat16):
    result = jax.random.normal(rng, dims, jnp.float32) * deviation
    if len(cuts) > 0:
        result = level_of(rng, dims, cuts, -0.22, 0.18) * result
    return jnp.clip(result, min=-limit, max=limit).astype(kind)


def setup_inputs(seed: int = 0) -> dict:
    seeds = jax.random.split(jax.random.key(seed), 9)
    acts = gaussian(seeds[0], (TOKENS, D), 0.5, 3.0, ((0, 256),))
    out_grads = gaussian(seeds[1], (TOKENS, D), 1.0, 6.0, ((0, 256),))
    token_counts = draw_token_counts(jax.random.fold_in(seeds[8], 71), 0)
    k_factor = draw_k_factor(jax.random.fold_in(seeds[8], 71), 0)
    c_factor = draw_c_factor(jax.random.fold_in(seeds[8], 71), 0)
    k_moment = draw_k_moment(jax.random.fold_in(seeds[8], 71), 0)
    c_moment = draw_c_moment(jax.random.fold_in(seeds[8], 71), 0)
    grad_weight = gaussian(seeds[7], (D, D), 1.0, 6.0, ((0, 8), (1, 32)))
    return dict(acts=acts, out_grads=out_grads, token_counts=token_counts, k_factor=k_factor, c_factor=c_factor, k_moment=k_moment, c_moment=c_moment, grad_weight=grad_weight)


damping = 0.1
momentum_rate = 0.5
step_rate = 0.2
highest = lax.Precision.HIGHEST


def statistics(masked, factor, border_keep, token_total):
    diag_half = factor[:, :, :BS].astype(jnp.bfloat16)
    side_half = (factor[:, :, BS:] * border_keep).astype(jnp.bfloat16)
    lead_columns = masked[:, :BS]
    lead_image = jnp.dot(lead_columns, diag_half[0], preferred_element_type=jnp.float32).astype(jnp.bfloat16)

    def one_block(block_index):
        columns = lax.dynamic_slice_in_dim(masked, block_index * BS, BS, 1)
        image_sum = jnp.dot(columns, diag_half[block_index], preferred_element_type=jnp.float32)
        image_sum = image_sum + jnp.dot(lead_columns, side_half[block_index], preferred_element_type=jnp.float32)
        image_block = image_sum.astype(jnp.bfloat16)
        own_sum = jnp.dot(image_block.T, image_block, preferred_element_type=jnp.float32) / token_total
        cross_sum = jnp.dot(lead_image.T, image_block, preferred_element_type=jnp.float32) / token_total
        return own_sum, cross_sum

    return lax.map(one_block, jnp.arange(NB, dtype=jnp.int32))


def gram_trace(factor, border_keep):
    diag_part = factor[:, :, :BS]
    side_part = factor[:, :, BS:] * border_keep
    return jnp.sum(diag_part * diag_part) + jnp.sum(side_part * side_part)


def advance(factor, moment, own_sum, cross_sum, lead_block, border_keep, other_h, other_g, width):
    diag_part = factor[:, :, :BS]
    side_part = factor[:, :, BS:] * border_keep
    gram_diag = jnp.einsum("nki,nkj->nij", diag_part, diag_part, precision=highest)
    gram_diag = gram_diag + jnp.einsum("nki,nkj->nij", side_part, side_part, precision=highest)
    gram_side = jnp.einsum("ki,nkj->nij", lead_block, side_part, precision=highest)
    identity = jnp.eye(BS, dtype=jnp.float32)
    fresh_diag = (other_h * own_sum + damping * other_g * gram_diag - width * identity) / (2.0 * width)
    fresh_side = (other_h * cross_sum + damping * other_g * gram_side) * border_keep / (2.0 * width)
    moment_diag = momentum_rate * moment[:, :, :BS] + fresh_diag
    moment_side = (momentum_rate * moment[:, :, BS:] + fresh_side) * border_keep
    new_diag = diag_part - step_rate * jnp.einsum("nik,nkj->nij", diag_part, moment_diag, precision=highest)
    side_change = jnp.einsum("ik,nkj->nij", lead_block, moment_side, precision=highest)
    side_change = side_change + jnp.einsum("nik,nkj->nij", side_part, moment_diag, precision=highest)
    new_side = (side_part - step_rate * side_change) * border_keep
    return jnp.concatenate([new_diag, new_side], axis=-1), jnp.concatenate([moment_diag, moment_side], axis=-1)


def precondition(grad_weight, k_new, c_new):
    k_diag = k_new[:, :, :BS].astype(jnp.bfloat16)
    k_side = k_new[:, :, BS:].astype(jnp.bfloat16)
    c_diag = c_new[:, :, :BS].astype(jnp.bfloat16)
    c_side = c_new[:, :, BS:].astype(jnp.bfloat16)
    block_range = jnp.arange(NB, dtype=jnp.int32)
    lead_columns = grad_weight[:, :BS]

    def first_block(block_index):
        columns = lax.dynamic_slice_in_dim(grad_weight, block_index * BS, BS, 1)
        total_sum = jnp.dot(columns, k_diag[block_index], preferred_element_type=jnp.float32)
        total_sum = total_sum + jnp.dot(lead_columns, k_side[block_index], preferred_element_type=jnp.float32)
        return total_sum.astype(jnp.bfloat16)

    first_product = lax.map(first_block, block_range)

    def second_block(block_index):
        return jnp.dot(first_product[block_index], k_diag[block_index].T, preferred_element_type=jnp.float32)

    own_second = lax.map(second_block, block_range)

    def add_lead(carry, block_index):
        return carry + jnp.dot(first_product[block_index], k_side[block_index].T, preferred_element_type=jnp.float32), None

    lead_term, unused = lax.scan(add_lead, jnp.zeros((D, BS), jnp.float32), block_range)
    second_product = own_second.at[0].add(lead_term).astype(jnp.bfloat16)
    by_rows = second_product.transpose(1, 0, 2).reshape(D, D).reshape(NB, BS, D)
    lead_rows = by_rows[0]

    def third_block(block_index):
        total_sum = jnp.dot(c_diag[block_index].T, by_rows[block_index], preferred_element_type=jnp.float32)
        total_sum = total_sum + jnp.dot(c_side[block_index].T, lead_rows, preferred_element_type=jnp.float32)
        return total_sum.astype(jnp.bfloat16)

    third_product = lax.map(third_block, block_range)

    def fourth_block(block_index):
        return jnp.dot(c_diag[block_index], third_product[block_index], preferred_element_type=jnp.float32)

    own_fourth = lax.map(fourth_block, block_range)

    def add_row(carry, block_index):
        return carry + jnp.dot(c_side[block_index], third_product[block_index], preferred_element_type=jnp.float32), None

    row_term, unused_rows = lax.scan(add_row, jnp.zeros((BS, D), jnp.float32), block_range)
    return own_fourth.at[0].add(row_term).astype(jnp.bfloat16).reshape(D, D)


def reference(acts, out_grads, token_counts, k_factor, c_factor, k_moment, c_moment, grad_weight):
    row_ids = jnp.arange(acts.shape[0], dtype=jnp.int32)
    group_of = row_ids // GROUP_TOK
    slot_of = row_ids % GROUP_TOK
    row_keep = (slot_of < token_counts[group_of]).astype(jnp.bfloat16)[:, None]
    masked_acts = acts * row_keep
    masked_grads = out_grads * row_keep
    token_total = jnp.sum(token_counts).astype(jnp.float32)
    border_keep = (jnp.arange(NB, dtype=jnp.int32) > 0).astype(jnp.float32)[:, None, None]
    own_k, cross_k = statistics(masked_acts, k_factor, border_keep, token_total)
    own_c, cross_c = statistics(masked_grads, c_factor, border_keep, token_total)
    trace_hk = jnp.sum(jnp.trace(own_k, axis1=1, axis2=2))
    trace_hc = jnp.sum(jnp.trace(own_c, axis1=1, axis2=2))
    trace_gk = gram_trace(k_factor, border_keep)
    trace_gc = gram_trace(c_factor, border_keep)
    width = float(D)
    k_factor_new, k_moment_new = advance(k_factor, k_moment, own_k, cross_k, k_factor[0, :, :BS], border_keep, trace_hc, trace_gc, width)
    c_factor_new, c_moment_new = advance(c_factor, c_moment, own_c, cross_c, c_factor[0, :, :BS], border_keep, trace_hk, trace_gk, width)
    precond = precondition(grad_weight, k_factor_new, c_factor_new)
    return (k_factor_new, c_factor_new, k_moment_new, c_moment_new, precond)
```

```python
import functools

import jax
import jax.numpy as jnp
from jax import lax
from jax.experimental import pallas as pl
from jax.experimental.pallas import tpu as pltpu
from jax.sharding import PartitionSpec as P

MESH = pl.DeviceIdType.MESH
highest = lax.Precision.HIGHEST
f32 = jnp.float32
bf16 = jnp.bfloat16

damping = 0.1
momentum_rate = 0.5
step_rate = 0.2

NX, NY, NZ = 4, 4, 8


def position():
    d = lax.axis_index("dp")
    f = lax.axis_index("fsdp")
    return lax.div(f, NZ), lax.div(d, 2), lax.rem(f, NZ), lax.rem(d, 2)


def device(x, y, z, c):
    return (y * 2 + c, x * NZ + z)


def class_of(x, y, z, c):
    return lax.rem(x, 2) * 8 + lax.rem(y, 2) * 4 + c * 2 + lax.rem(z, 2)


def send(src, dst, send_sem, recv_sem, target):
    return pltpu.make_async_remote_copy(
        src_ref=src, dst_ref=dst, send_sem=send_sem, recv_sem=recv_sem, device_id=target, device_id_type=MESH
    )


def arrived(dst, sem):
    pltpu.make_async_copy(dst, dst, sem).wait()


def greet(barrier, target):
    pl.semaphore_signal(barrier, inc=1, device_id=target, device_id_type=MESH)


ANY = pl.BlockSpec(memory_space=pl.ANY)
VM = pl.BlockSpec(memory_space=pltpu.VMEM)
DMA = pltpu.SemaphoreType.DMA


def call(body, name, ins, in_specs, outs, out_specs, scratch=(), cid=None):
    params = dict(collective_id=cid, has_side_effects=True) if cid is not None else {}
    return pl.pallas_call(
        body,
        out_shape=[jax.ShapeDtypeStruct(s, t) for s, t in outs],
        in_specs=in_specs,
        out_specs=out_specs,
        scratch_shapes=list(scratch),
        compiler_params=pltpu.CompilerParams(**params),
        name=name,
    )(*ins)


def token_body(acts, grads, keep, pieces, xc, x0, piece, xs, ls, s1, r1, s2, r2, s3, r3, l1, l2):
    x, y, z, c = position()
    d, f = lax.axis_index("dp"), lax.axis_index("fsdp")
    barrier = pltpu.get_barrier_semaphore()

    def at(sign, a, b, g, e):
        return (
            lax.rem(x + sign * a + NX, NX),
            lax.rem(y + sign * b + NY, NY),
            lax.rem(z + sign * g + NZ, NZ),
            lax.rem(c + e, 2),
        )

    offsets = [(a, b, g, e) for a in (0, 1) for b in (0, 1) for g in (0, 1) for e in (0, 1)]
    for sign in (1, -1):
        for o in offsets:
            if o[:3] == (0, 0, 0) and (o[3] == 0 or sign == -1):
                continue
            greet(barrier, device(*at(sign, *o)))

    @pl.when(f > 0)
    def _():
        greet(barrier, (d, 0))

    for side, ref in enumerate((acts, grads)):
        for h in range(2):
            rows = slice(h * 64, h * 64 + 64)
            kept = keep[rows, :]
            ls[h, side, :, :] = ref[rows, 0:256] * kept
            for k in range(16):
                for m in range(2):
                    n = m * 16 + k
                    xs[k, h, side, :, m * 256 : m * 256 + 256] = ref[rows, n * 256 : n * 256 + 256] * kept

    pl.semaphore_wait(barrier, 29 + jnp.where(f == 0, 31, 0))
    copies = []
    for h, sign in ((0, 1), (1, -1)):
        for i, o in enumerate(offsets):
            there = at(sign, *o)
            k = class_of(*there)
            slot = h * 16 + i
            if i == 0:
                one = pltpu.make_async_copy(xs.at[k, h], xc.at[:, slot], l1.at[h])
                two = pltpu.make_async_copy(ls.at[h], x0.at[:, slot], l2.at[h])
            else:
                one = send(xs.at[k, h], xc.at[:, slot], s1.at[slot], r1.at[slot], device(*there))
                two = send(ls.at[h], x0.at[:, slot], s2.at[slot], r2.at[slot], device(*there))
            one.start()
            two.start()
            copies += [one, two]

    @pl.when(f == 0)
    def _():
        own = pltpu.make_async_copy(pieces.at[0], piece, r3)
        own.start()

        @pl.loop(1, 32)
        def _(t):
            send(pieces.at[t], piece, s3.at[t], r3, (d, t)).start()

        @pl.loop(1, 32)
        def _(t):
            send(pieces.at[t], piece, s3.at[t], r3, (d, t)).wait_send()

    arrived(piece, r3)
    for one in copies:
        one.wait()


def gram_body(xc, x0, out):
    dims = (((0,), (0,)), ((), ()))
    for side in range(2):
        lead = x0[side]
        a = xc[side, :, 0:256]
        b = xc[side, :, 256:512]
        for i, (l, r) in enumerate(((a, a), (b, b), (lead, a), (lead, b), (lead, lead))):
            g = lax.dot_general(l, r, dims, preferred_element_type=f32)
            out[:, side * 5 + i, :, :] = g.astype(bf16).reshape(16, 16, 256)


def scatter_body(parts, out, s, r, l):
    x, y, z, c = position()
    barrier = pltpu.get_barrier_semaphore()
    offsets = [(a, b, g) for a in range(2) for b in range(2) for g in range(4)]

    def at(a, b, g):
        return lax.rem(x + 2 * a, NX), lax.rem(y + 2 * b, NY), lax.rem(z + 2 * g, NZ)

    for o in offsets[1:]:
        greet(barrier, device(*at(*o), c))
    pl.semaphore_wait(barrier, 15)
    copies = []
    for i, o in enumerate(offsets):
        tx, ty, tz = at(*o)
        j = lax.div(tx, 2) * 8 + lax.div(ty, 2) * 4 + lax.div(tz, 2)
        if i == 0:
            copy = pltpu.make_async_copy(parts.at[j], out.at[0], l)
        else:
            copy = send(parts.at[j], out.at[i], s.at[i], r.at[i], device(tx, ty, tz, c))
        copy.start()
        copies.append(copy)
    for copy in copies:
        copy.wait()


def sum_body(parts, out):
    total = parts[0].astype(f32)
    for i in range(1, 16):
        total = total + parts[i].astype(f32)
    total = total.astype(bf16)
    for m in range(2):
        for side in range(2):
            for q, source in enumerate((m, 2 + m, 4)):
                out[m, side * 3 + q] = total[side * 5 + source]


def deliver_body(rows, out, s, r):
    x, y, z, c = position()
    d, f = lax.axis_index("dp"), lax.axis_index("fsdp")
    barrier = pltpu.get_barrier_semaphore()
    mine = class_of(x, y, z, c)
    slot = lax.div(x, 2) * 8 + lax.div(y, 2) * 4 + lax.div(z, 2)
    k = lax.rem(f, 16)
    px, py, pc, pz = lax.div(k, 8), lax.rem(lax.div(k, 4), 2), lax.rem(lax.div(k, 2), 2), lax.rem(k, 2)
    own = jnp.where(mine == k, 1, 0)

    def source(j):
        return device(px + 2 * lax.div(j, 8), py + 2 * lax.rem(lax.div(j, 4), 2), pz + 2 * lax.rem(j, 4), pc)

    def is_me(there):
        return jnp.logical_and(there[0] == d, there[1] == f)

    @pl.loop(0, 16)
    def _(j):
        there = source(j)

        @pl.when(jnp.logical_not(is_me(there)))
        def _():
            greet(barrier, there)

    pl.semaphore_wait(barrier, 16 - own)

    @pl.loop(0, 16)
    def _(t):
        m = lax.div(t, 8)
        there = (lax.rem(t, 8), mine + 16 * m)

        @pl.when(is_me(there))
        def _():
            pltpu.make_async_copy(rows.at[m], out.at[slot], r.at[slot]).start()

        @pl.when(jnp.logical_not(is_me(there)))
        def _():
            send(rows.at[m], out.at[slot], s.at[t], r.at[slot], there).start()

    @pl.loop(0, 16)
    def _(t):
        m = lax.div(t, 8)
        there = (lax.rem(t, 8), mine + 16 * m)

        @pl.when(jnp.logical_not(is_me(there)))
        def _():
            send(rows.at[m], out.at[slot], s.at[t], r.at[slot], there).wait_send()

    @pl.loop(0, 16)
    def _(j):
        arrived(out.at[j], r.at[j])


def dot(a, b):
    return jnp.dot(a, b, precision=highest, preferred_element_type=f32)


def dot16(a, b):
    return jnp.dot(a, b, preferred_element_type=f32)


def second_moment_body(stats, k_factor, c_factor, keep, u_out, h_out, tr_out):
    flag = keep[0:1, 0:1]
    rows = lax.broadcasted_iota(jnp.int32, (256, 256), 0)
    cols = lax.broadcasted_iota(jnp.int32, (256, 256), 1)
    for side, factor in enumerate((k_factor, c_factor)):
        a = stats[:, side * 3 + 0].reshape(256, 256)
        cross = stats[:, side * 3 + 1].reshape(256, 256)
        lead = stats[:, side * 3 + 2].reshape(256, 256)
        diag = factor[0, :, 0:256]
        border = factor[0, :, 256:512] * flag
        diag16, border16 = diag.astype(bf16), border.astype(bf16)
        u = dot16(cross, diag16) + dot16(lead, border16)
        v = dot16(a, diag16) + dot16(cross.T, border16)
        h = dot(diag16.astype(f32).T, v) + dot(border16.astype(f32).T, u)
        u_out[side] = u
        h_out[side] = h
        tr_h = jnp.sum(jnp.where(rows == cols, h, 0.0))
        tr_g = jnp.sum(diag * diag) + jnp.sum(border * border)
        tr_out[side * 2 : side * 2 + 1, :] = jnp.full((1, 128), tr_h, f32)
        tr_out[side * 2 + 1 : side * 2 + 2, :] = jnp.full((1, 128), tr_g, f32)
    tr_out[4:8, :] = jnp.zeros((4, 128), f32)


def gather_body(count, *refs):
    ins, outs, sems = refs[:count], refs[count : 2 * count], refs[2 * count :]
    d, f = lax.axis_index("dp"), lax.axis_index("fsdp")
    barrier = pltpu.get_barrier_semaphore()

    @pl.loop(1, 32)
    def _(t):
        greet(barrier, (d, lax.rem(f + t, 32)))

    pl.semaphore_wait(barrier, 31)
    for i in range(count):
        s, r = sems[2 * i], sems[2 * i + 1]
        pltpu.make_async_copy(ins[i], outs[i].at[f], r.at[0]).start()

        @pl.loop(1, 32)
        def _(t):
            send(ins[i], outs[i].at[f], s.at[t], r.at[t], (d, lax.rem(f + t, 32))).start()

    for i in range(count):
        s, r = sems[2 * i], sems[2 * i + 1]
        arrived(outs[i].at[f], r.at[0])

        @pl.loop(1, 32)
        def _(t):
            send(ins[i], outs[i].at[f], s.at[t], r.at[t], (d, lax.rem(f + t, 32))).wait_send()
            arrived(outs[i].at[lax.rem(f + 32 - t, 32)], r.at[t])


def gather(ins, cid, name):
    n = len(ins)
    return call(
        functools.partial(gather_body, n),
        name,
        ins,
        [ANY] * n,
        [((32,) + v.shape, v.dtype) for v in ins],
        [ANY] * n,
        [DMA((32,))] * (2 * n),
        cid,
    )


def advance_body(
    tr, total, keep, h_in, u_in, k_factor, c_factor, k_moment, c_moment, lead_pieces, grad, k_new, c_new, km_new, cm_new,
    c_half, own_out, lead_out,
):
    flag = keep[0:1, 0:1]
    inverse = 1.0 / total[0:1, 0:1]
    width = 8192.0
    sums = tr[0]
    for i in range(1, 32):
        sums = sums + tr[i]
    trace = [sums[i : i + 1, 0:1] for i in range(4)]
    rows = lax.broadcasted_iota(jnp.int32, (256, 256), 0)
    cols = lax.broadcasted_iota(jnp.int32, (256, 256), 1)
    identity = jnp.where(rows == cols, 1.0, 0.0)
    halves = []
    for side, (factor, moment, f_new, m_new) in enumerate(
        ((k_factor, k_moment, k_new, km_new), (c_factor, c_moment, c_new, cm_new))
    ):
        other_h = trace[2 - 2 * side] * inverse * inverse
        other_g = trace[3 - 2 * side] * damping
        diag = factor[0, :, 0:256]
        border = factor[0, :, 256:512] * flag
        lead = lead_pieces[:, side * 8 : side * 8 + 8].reshape(256, 256).astype(f32)
        gram = dot(diag.T, diag) + dot(border.T, border)
        fresh = (other_h * h_in[side] + other_g * gram - width * identity) / (2.0 * width)
        cross = dot(lead.T, other_h * u_in[side] + other_g * border) * flag / (2.0 * width)
        m_diag = momentum_rate * moment[0, :, 0:256] + fresh
        m_side = (momentum_rate * moment[0, :, 256:512] + cross) * flag
        n_diag = diag - step_rate * dot(diag, m_diag)
        n_side = (border - step_rate * (dot(lead, m_side) + dot(border, m_diag))) * flag
        f_new[0, :, 0:256] = n_diag
        f_new[0, :, 256:512] = n_side
        m_new[0, :, 0:256] = m_diag
        m_new[0, :, 256:512] = m_side
        halves.append((n_diag.astype(bf16), n_side.astype(bf16)))
    k_diag, k_side = halves[0]
    c_half[0:256, :] = halves[1][0]
    c_half[256:512, :] = halves[1][1]
    grad_lead = lead_pieces[:, 16:48].reshape(1024, 256)
    first = (dot16(grad[...], k_diag) + dot16(grad_lead, k_side)).astype(bf16)
    own_out[...] = dot16(first, k_diag.T)
    lead_out[...] = dot16(first, k_side.T).astype(bf16).reshape(32, 32, 256)


def border_body(lead, c_half, parts, c_part, s, r, s2, r2, l):
    d, f = lax.axis_index("dp"), lax.axis_index("fsdp")
    barrier = pltpu.get_barrier_semaphore()
    own = pltpu.make_async_copy(lead.at[f], parts.at[f], l)
    own.start()

    @pl.loop(1, 32)
    def _(t):
        greet(barrier, (d, lax.rem(f + t, 32)))

    pl.semaphore_wait(barrier, 31)
    root = lax.div(f, 4) == d
    q = lax.rem(f, 4)

    @pl.loop(1, 32)
    def _(t):
        there = lax.rem(f + t, 32)
        send(lead.at[there], parts.at[f], s.at[t], r.at[t], (d, there)).start()

    @pl.when(root)
    def _():
        pltpu.make_async_copy(c_half.at[pl.ds(pl.multiple_of(f * 16, 16), 16)], c_part.at[q], r2.at[q]).start()

        @pl.loop(1, 32)
        def _(t):
            there = lax.rem(f + t, 32)
            src = c_half.at[pl.ds(pl.multiple_of(there * 16, 16), 16)]
            send(src, c_part.at[q], s2.at[t], r2.at[q], (d, there)).start()

    own.wait()

    @pl.loop(1, 32)
    def _(t):
        there = lax.rem(f + t, 32)
        send(lead.at[there], parts.at[f], s.at[t], r.at[t], (d, there)).wait_send()
        arrived(parts.at[lax.rem(f + 32 - t, 32)], r.at[t])

    @pl.when(root)
    def _():
        @pl.loop(1, 32)
        def _(t):
            there = lax.rem(f + t, 32)
            src = c_half.at[pl.ds(pl.multiple_of(there * 16, 16), 16)]
            send(src, c_part.at[q], s2.at[t], r2.at[q], (d, there)).wait_send()

    for j in range(4):
        arrived(c_part.at[j], r2.at[j])


def border_sum_body(parts, out):
    total = parts[0].astype(f32)
    for i in range(1, 32):
        total = total + parts[i].astype(f32)
    out[...] = total.astype(bf16)


def factors_body(c_part, lead, all_c, all_lead, s, r, s2, r2):
    d, f = lax.axis_index("dp"), lax.axis_index("fsdp")
    barrier = pltpu.get_barrier_semaphore()

    @pl.loop(1, 32)
    def _(t):
        greet(barrier, (d, lax.rem(f + t, 32)))

    pl.semaphore_wait(barrier, 31)

    @pl.when(f > 0)
    def _():
        send(lead, all_lead.at[f], s2, r2.at[f], (d, 0)).start()

    @pl.when(f == 0)
    def _():
        pltpu.make_async_copy(lead, all_lead.at[0], r2.at[0]).start()

    pltpu.make_async_copy(c_part, all_c.at[f], r.at[0]).start()

    @pl.loop(1, 32)
    def _(t):
        send(c_part, all_c.at[f], s.at[t], r.at[t], (d, lax.rem(f + t, 32))).start()

    arrived(all_c.at[f], r.at[0])

    @pl.loop(1, 32)
    def _(t):
        send(c_part, all_c.at[f], s.at[t], r.at[t], (d, lax.rem(f + t, 32))).wait_send()
        arrived(all_c.at[lax.rem(f + 32 - t, 32)], r.at[t])

    @pl.when(f > 0)
    def _():
        send(lead, all_lead.at[f], s2, r2.at[f], (d, 0)).wait_send()

    @pl.when(f == 0)
    def _():
        @pl.loop(0, 32)
        def _(t):
            arrived(all_lead.at[t], r2.at[t])


def second_body(first_flag, own, lead, out):
    kept = jnp.where(first_flag[0:1, 0:1] > 0.0, lead[...].reshape(1024, 256).astype(f32), 0.0)
    out[...] = (own[...] + kept).astype(bf16)


def rows_body(second, out, s, r):
    d, f = lax.axis_index("dp"), lax.axis_index("fsdp")
    barrier = pltpu.get_barrier_semaphore()
    src = second.at[0:256]

    @pl.when(d > 0)
    def _():
        greet(barrier, (0, f))
        arrived(out, r)

    @pl.when(d == 0)
    def _():
        pl.semaphore_wait(barrier, 7)
        pltpu.make_async_copy(src, out, r).start()
        for t in range(1, 8):
            send(src, out, s.at[t], r, (t, f)).start()
        arrived(out, r)
        for t in range(1, 8):
            send(src, out, s.at[t], r, (t, f)).wait_send()


def third_body(second, lead_rows, pieces, own_out, term_out):
    term = jnp.zeros((256, 256), f32)
    for j in range(4):
        diag = pieces[0:16, j].reshape(256, 256)
        side = pieces[16:32, j].reshape(256, 256)
        third = dot16(diag.T, second[j * 256 : j * 256 + 256, :]) + dot16(side.T, lead_rows[...])
        third = third.astype(bf16)
        own_out[j * 256 : j * 256 + 256, :] = dot16(diag, third)
        term = term + dot16(side, third)
    term_out[...] = term.astype(bf16)


def term_body(term, out, s, r, l):
    d, f = lax.axis_index("dp"), lax.axis_index("fsdp")
    barrier = pltpu.get_barrier_semaphore()

    @pl.when(d > 0)
    def _():
        pl.semaphore_wait(barrier, 1)
        copy = send(term, out.at[d], s, r.at[d], (0, f))
        copy.start()
        copy.wait_send()

    @pl.when(d == 0)
    def _():
        for t in range(1, 8):
            greet(barrier, (t, f))
        own = pltpu.make_async_copy(term, out.at[0], l)
        own.start()
        own.wait()
        for t in range(1, 8):
            arrived(out.at[t], r.at[t])


def final_body(flag, own, terms, out):
    total = jnp.zeros((256, 256), f32)
    kept = flag[0:1, 0:1] > 0.0
    for i in range(8):
        total = total + terms[i].astype(f32)
    out[0:256, :] = (own[0:256, :] + jnp.where(kept, total, 0.0)).astype(bf16)
    out[256:1024, :] = own[256:1024, :].astype(bf16)


def per_device(acts, out_grads, token_counts, k_factor, c_factor, k_moment, c_moment, grad_weight):
    d = lax.axis_index("dp")
    f = lax.axis_index("fsdp")
    token_total = jnp.broadcast_to(jnp.sum(token_counts).astype(f32), (8, 128))
    limit = jnp.sum(jnp.where(lax.iota(jnp.int32, 8) == d, token_counts, 0))
    keep = (f * 128 + lax.broadcasted_iota(jnp.int32, (128, 256), 0) < limit).astype(bf16)
    border_keep = jnp.broadcast_to((f > 0).astype(f32), (8, 128))
    first_column = jnp.broadcast_to((f == 0).astype(f32), (8, 128))
    first_row = jnp.broadcast_to((d == 0).astype(f32), (8, 128))
    pieces = jnp.concatenate(
        [
            k_factor[0, :, :256].astype(bf16).reshape(32, 8, 256),
            c_factor[0, :, :256].astype(bf16).reshape(32, 8, 256),
            grad_weight.reshape(32, 32, 256),
        ],
        axis=1,
    )
    xc, x0, piece = call(
        token_body, "tokens", (acts, out_grads, keep, pieces), [VM, VM, VM, ANY],
        [((2, 32, 64, 512), bf16), ((2, 32, 64, 256), bf16), ((48, 256), bf16)], [ANY, ANY, ANY],
        [pltpu.VMEM((16, 2, 2, 64, 512), bf16), pltpu.VMEM((2, 2, 64, 256), bf16)]
        + [DMA((32,))] * 4 + [DMA((32,)), DMA, DMA((2,)), DMA((2,))],
        0,
    )
    (parts,) = call(
        gram_body, "gram", (xc.reshape(2, 2048, 512), x0.reshape(2, 2048, 256)), [VM, VM],
        [((16, 10, 16, 256), bf16)], [VM],
    )
    (shares,) = call(
        scatter_body, "scatter", (parts,), [ANY], [((16, 10, 16, 256), bf16)], [ANY], [DMA((16,)), DMA((16,)), DMA], 1
    )
    (rows,) = call(sum_body, "sum", (shares,), [VM], [((2, 6, 16, 256), bf16)], [VM])
    (stats,) = call(
        deliver_body, "deliver", (rows,), [ANY], [((16, 6, 16, 256), bf16)], [ANY], [DMA((16,)), DMA((16,))], 2
    )
    u, h, traces = call(
        second_moment_body, "moments", (stats, k_factor, c_factor, border_keep), [VM] * 4,
        [((2, 256, 256), f32), ((2, 256, 256), f32), ((8, 128), f32)], [VM] * 3,
    )
    all_traces, lead_pieces = gather((traces, piece), 3, "traces")
    k_new, c_new, km_new, cm_new, c_half, own_second, lead_term = call(
        advance_body, "advance",
        (all_traces, token_total, border_keep, h, u, k_factor, c_factor, k_moment, c_moment, lead_pieces, grad_weight),
        [VM] * 11,
        [((1, 256, 512), f32)] * 4
        + [((512, 256), bf16), ((1024, 256), f32), ((32, 32, 256), bf16)],
        [VM] * 7,
    )
    lead_parts, c_part = call(
        border_body, "border", (lead_term, c_half), [ANY, ANY],
        [((32, 32, 256), bf16), ((4, 16, 256), bf16)], [ANY, ANY],
        [DMA((32,)), DMA((32,)), DMA((32,)), DMA((4,)), DMA], 4,
    )
    (lead_rows32,) = call(border_sum_body, "border_sum", (lead_parts,), [VM], [((32, 256), bf16)], [VM])
    all_c, all_lead = call(
        factors_body, "factors", (c_part, lead_rows32), [ANY, ANY],
        [((32, 4, 16, 256), bf16), ((32, 32, 256), bf16)], [ANY, ANY],
        [DMA((32,)), DMA((32,)), DMA, DMA((32,))], 5,
    )
    (second,) = call(
        second_body, "second", (first_column, own_second, all_lead), [VM] * 3, [((1024, 256), bf16)], [VM]
    )
    (lead_rows,) = call(
        rows_body, "rows", (second,), [ANY], [((256, 256), bf16)], [ANY], [DMA((8,)), DMA], 6
    )
    own_fourth, term = call(
        third_body, "third", (second, lead_rows, all_c), [VM] * 3,
        [((1024, 256), f32), ((256, 256), bf16)], [VM] * 2,
    )
    (terms,) = call(
        term_body, "terms", (term,), [ANY], [((8, 256, 256), bf16)], [ANY], [DMA, DMA((8,)), DMA], 7
    )
    (precond,) = call(final_body, "final", (first_row, own_fourth, terms), [VM] * 3, [((1024, 256), bf16)], [VM])
    return k_new, c_new, km_new, cm_new, precond


def solution(mesh):
    in_specs = (
        P(("dp", "fsdp"), None),
        P(("dp", "fsdp"), None),
        P(),
        P("fsdp", None, None),
        P("fsdp", None, None),
        P("fsdp", None, None),
        P("fsdp", None, None),
        P("dp", "fsdp"),
    )
    out_specs = (
        P("fsdp", None, None),
        P("fsdp", None, None),
        P("fsdp", None, None),
        P("fsdp", None, None),
        P("dp", "fsdp"),
    )
    return jax.shard_map(per_device, mesh=mesh, in_specs=in_specs, out_specs=out_specs, check_vma=False)
```

```python
import functools

import jax
import jax.numpy as jnp
from jax import lax
from jax.experimental import pallas as pl
from jax.experimental.pallas import tpu as pltpu
from jax.sharding import PartitionSpec as P

MESH = pl.DeviceIdType.MESH
highest = lax.Precision.HIGHEST
f32 = jnp.float32
bf16 = jnp.bfloat16

damping = 0.1
momentum_rate = 0.5
step_rate = 0.2

NX, NY, NZ = 4, 4, 8


def position():
    d = lax.axis_index("dp")
    f = lax.axis_index("fsdp")
    return lax.div(f, NZ), lax.div(d, 2), lax.rem(f, NZ), lax.rem(d, 2)


def device(x, y, z, c):
    return (y * 2 + c, x * NZ + z)


def class_of(x, y, z, c):
    return lax.rem(x, 2) * 8 + lax.rem(y, 2) * 4 + c * 2 + lax.rem(z, 2)


def send(src, dst, send_sem, recv_sem, target):
    return pltpu.make_async_remote_copy(
        src_ref=src, dst_ref=dst, send_sem=send_sem, recv_sem=recv_sem, device_id=target, device_id_type=MESH
    )


def arrived(dst, sem):
    pltpu.make_async_copy(dst, dst, sem).wait()


def greet(barrier, target):
    pl.semaphore_signal(barrier, inc=1, device_id=target, device_id_type=MESH)


ANY = pl.BlockSpec(memory_space=pl.ANY)
VM = pl.BlockSpec(memory_space=pltpu.VMEM)
DMA = pltpu.SemaphoreType.DMA


def call(body, name, ins, in_specs, outs, out_specs, scratch=(), cid=None):
    params = dict(collective_id=cid, has_side_effects=True) if cid is not None else {}
    return pl.pallas_call(
        body,
        out_shape=[jax.ShapeDtypeStruct(s, t) for s, t in outs],
        in_specs=in_specs,
        out_specs=out_specs,
        scratch_shapes=list(scratch),
        compiler_params=pltpu.CompilerParams(**params),
        name=name,
    )(*ins)


def token_body(
    counts, acts, grads, k_factor, c_factor, grad, xc, x0, piece_b, piece_g,
    xs, ls, b0, s1, r1, s2, r2, s3, r3, l1, s4, s5, r4,
):
    x, y, z, c = position()
    d, f = lax.axis_index("dp"), lax.axis_index("fsdp")
    barrier = pltpu.get_barrier_semaphore()

    def at(sign, a, b, g, e):
        return (
            lax.rem(x + sign * a + NX, NX),
            lax.rem(y + sign * b + NY, NY),
            lax.rem(z + sign * g + NZ, NZ),
            lax.rem(c + e, 2),
        )

    offsets = [(a, b, g, e) for a in (0, 1) for b in (0, 1) for g in (0, 1) for e in (0, 1)]
    for sign in (1, -1):
        for o in offsets:
            if o[:3] == (0, 0, 0) and (o[3] == 0 or sign == -1):
                continue
            greet(barrier, device(*at(sign, *o)))

    @pl.when(f > 0)
    def _():
        greet(barrier, (d, 0))

    limit = counts[0] * jnp.where(d == 0, 1, 0)
    for i in range(1, 8):
        limit = limit + counts[i] * jnp.where(d == i, 1, 0)
    for h in range(2):
        rows = slice(h * 64, h * 64 + 64)
        slots = lax.broadcasted_iota(jnp.int32, (64, 256), 0) + (f * 128 + h * 64)
        kept = jnp.where(slots < limit, 1.0, 0.0).astype(bf16)
        for side, ref in enumerate((acts, grads)):
            lead = ref[rows, 0:256] * kept
            ls[0, h, side, :, :] = lead[:, 0:128]
            ls[1, h, side, :, :] = lead[:, 128:256]
            for k in range(16):
                for m in range(2):
                    n = m * 16 + k
                    xs[k, h, side, :, m * 256 : m * 256 + 256] = ref[rows, n * 256 : n * 256 + 256] * kept

    @pl.when(f == 0)
    def _():
        b0[0:256, :] = k_factor[0, :, 0:256].astype(bf16)
        b0[256:512, :] = c_factor[0, :, 0:256].astype(bf16)

    pl.semaphore_wait(barrier, 29 + jnp.where(f == 0, 31, 0))
    half = pl.ds(pl.multiple_of(c * 128, 128), 128)
    other_half = pl.ds(pl.multiple_of(128 - c * 128, 128), 128)
    partner = device(x, y, z, 1 - c)
    copies, leads = [], []
    for i in (14, 15, 12, 13, 10, 11, 6, 7, 8, 9, 4, 5, 2, 3, 1, 0):
        for h, sign in ((0, 1), (1, -1)):
            o = offsets[i]
            there = at(sign, *o)
            k = class_of(*there)
            slot = h * 16 + i
            if i == 0:
                one = pltpu.make_async_copy(xs.at[k, h], xc.at[:, slot], l1.at[h])
                two = pltpu.make_async_copy(ls.at[c, h], x0.at[:, slot, :, half], r2.at[slot])
            else:
                tc = there[3]
                to_half = pl.ds(pl.multiple_of(tc * 128, 128), 128)
                one = send(xs.at[k, h], xc.at[:, slot], s1.at[slot], r1.at[slot], device(*there))
                two = send(ls.at[tc, h], x0.at[:, slot, :, to_half], s2.at[slot], r2.at[slot], device(*there))
            two.start()
            one.start()
            copies.append(one)
            leads.append((i, slot, two))

    def grad_piece(t):
        return grad.at[pl.ds(pl.multiple_of(t * 32, 32), 32)]

    def lead_piece(t):
        return b0.at[pl.ds(pl.multiple_of(t * 16, 16), 16)]

    @pl.when(f == 0)
    def _():
        pltpu.make_async_copy(grad_piece(0), piece_g, r3.at[0]).start()
        pltpu.make_async_copy(lead_piece(0), piece_b, r3.at[1]).start()

        @pl.loop(1, 32)
        def _(t):
            send(grad_piece(t), piece_g, s3.at[t], r3.at[0], (d, t)).start()
            send(lead_piece(t), piece_b, s4.at[t], r3.at[1], (d, t)).start()

    passed = []
    for i, slot, two in leads:
        mine = x0.at[:, slot, :, half]
        arrived(mine, r2.at[slot])
        on = send(mine, x0.at[:, slot ^ 1, :, half], s5.at[slot], r4.at[slot ^ 1], partner)
        on.start()
        passed.append(on)
    for i, slot, two in leads:
        if i > 0:
            two.wait_send()
    for slot, on in zip([slot for _, slot, _ in leads], passed):
        on.wait_send()
        arrived(x0.at[:, slot, :, other_half], r4.at[slot])
    for one in copies:
        one.wait()
    arrived(piece_g, r3.at[0])
    arrived(piece_b, r3.at[1])

    @pl.when(f == 0)
    def _():
        @pl.loop(1, 32)
        def _(t):
            send(grad_piece(t), piece_g, s3.at[t], r3.at[0], (d, t)).wait_send()
            send(lead_piece(t), piece_b, s4.at[t], r3.at[1], (d, t)).wait_send()


def dot(a, b):
    return jnp.dot(a, b, precision=highest, preferred_element_type=f32)


def dot16(a, b):
    return jnp.dot(a, b, preferred_element_type=f32)


def stats_body(
    xc, x0, k_factor, c_factor, piece_b, piece_g, h_out, u_out, gram_out, tr_out, b0_out, g0_out,
    ps, pi, sm, st, tr, lead_b, lead_g,
    rs_s, rs_r, de_s, de_r, ag_s, zb_s, zb_r, zg_s, zg_r, xb_s, xb_r, xg_s, xg_r, tr_s, tr_r,
):
    x, y, z, c = position()
    d, f = lax.axis_index("dp"), lax.axis_index("fsdp")
    barrier = pltpu.get_barrier_semaphore()
    mine = class_of(x, y, z, c)
    xi, yi, zi = lax.div(x, 2), lax.div(y, 2), lax.div(z, 2)
    slot = xi * 8 + yi * 4 + zi
    mates = [(a, b, g) for a in range(2) for b in range(2) for g in range(4)]

    def mate(a, b, g):
        return lax.rem(x + 2 * a, NX), lax.rem(y + 2 * b, NY), lax.rem(z + 2 * g, NZ)

    to_d = lax.rem(y + lax.rem(zi, 2), NY) * 2 + lax.div(zi, 2)
    k = lax.rem(f, 16)
    px, py, pc, pz = lax.div(k, 8), lax.rem(lax.div(k, 4), 2), lax.rem(lax.div(k, 2), 2), lax.rem(k, 2)
    shift = lax.rem(y + py, 2)
    from_y = lax.rem(y - shift + NY, NY)
    from_zi = 2 * c + shift
    from_j = [i * 8 + lax.div(from_y, 2) * 4 + from_zi for i in range(2)]
    from_at = [device(px + 2 * i, from_y, pz + 2 * from_zi, pc) for i in range(2)]

    def is_me(there):
        return jnp.logical_and(there[0] == d, there[1] == f)

    for o in mates[1:]:
        greet(barrier, device(*mate(*o), c))

    @pl.loop(1, 32)
    def _(t):
        greet(barrier, (d, lax.rem(f + t, 32)))

    for t in range(1, 8):
        greet(barrier, (lax.rem(d + t, 8), f))
    for there in from_at:

        @pl.when(jnp.logical_not(is_me(there)))
        def _():
            greet(barrier, there)

    dims = (((0,), (0,)), ((), ()))

    def gram(side):
        lead = x0[side]
        a = xc[side, :, 0:256]
        b = xc[side, :, 256:512]
        for i, (left, right) in enumerate(((a, a), (b, b), (lead, a), (lead, b), (lead, lead))):
            g = lax.dot_general(left, right, dims, preferred_element_type=f32)
            ps[side, :, i, :, :] = g.astype(bf16).reshape(16, 16, 256)

    def scatter(side):
        copies = []
        for i, o in enumerate(mates):
            if i > 0:
                tx, ty, tz = mate(*o)
                j = lax.div(tx, 2) * 8 + lax.div(ty, 2) * 4 + lax.div(tz, 2)
                copy = send(ps.at[side, j], pi.at[side, i], rs_s.at[side, i], rs_r.at[side, i], device(tx, ty, tz, c))
                copy.start()
                copies.append(copy)
        return copies

    gram(0)
    to_self = jnp.where(is_me((to_d, mine)), 1, 0) + jnp.where(is_me((to_d, mine + 16)), 1, 0)
    pl.semaphore_wait(barrier, 15 + 31 + 7 + 2 - to_self)
    first = scatter(0)
    own_b = pltpu.make_async_copy(piece_b, lead_b.at[x, z], zb_r.at[0])
    own_g = pltpu.make_async_copy(piece_g, lead_g.at[x, z], zg_r.at[0])
    own_b.start()
    own_g.start()
    for t in range(1, 8):
        there = (d, x * NZ + lax.rem(z + t, NZ))
        send(piece_b, lead_b.at[x, z], zb_s.at[t], zb_r.at[t], there).start()
        send(piece_g, lead_g.at[x, z], zg_s.at[t], zg_r.at[t], there).start()
    gram(1)
    second = scatter(1)

    flag = jnp.where(f > 0, 1.0, 0.0)
    factors = []
    for side, factor in enumerate((k_factor, c_factor)):
        diag = factor[0, :, 0:256]
        border = factor[0, :, 256:512] * flag
        gram_out[side] = dot(diag.T, diag) + dot(border.T, border)
        factors.append((diag, border))

    def total(side, copies):
        for copy in copies:
            copy.wait()
        value = ps[side, slot].astype(f32)
        for i in range(1, 16):
            value = value + pi[side, i].astype(f32)
        value = value.astype(bf16)
        for m in range(2):
            for q, source in enumerate((m, 2 + m, 4)):
                sm[side, m, q] = value[source]

    def deliver(side):
        for m in range(2):
            there = (to_d, mine + 16 * m)

            @pl.when(is_me(there))
            def _():
                pltpu.make_async_copy(sm.at[side, m], st.at[side, slot], de_r.at[side, slot]).start()

            @pl.when(jnp.logical_not(is_me(there)))
            def _():
                send(sm.at[side, m], st.at[side, slot], de_s.at[side, m], de_r.at[side, slot], there).start()

    def share(side):
        for i in range(2):
            j = from_j[i]
            arrived(st.at[side, j], de_r.at[side, j])
            for t in range(1, 8):
                there = (lax.rem(d + t, 8), f)
                send(st.at[side, j], st.at[side, j], ag_s.at[side, i, t], de_r.at[side, j], there).start()

    total(0, first)
    deliver(0)
    own_b.wait()
    own_g.wait()
    for t in range(1, 8):
        there = (d, x * NZ + lax.rem(z + t, NZ))
        behind = lax.rem(z + NZ - t, NZ)
        send(piece_b, lead_b.at[x, z], zb_s.at[t], zb_r.at[t], there).wait_send()
        send(piece_g, lead_g.at[x, z], zg_s.at[t], zg_r.at[t], there).wait_send()
        arrived(lead_b.at[x, behind], zb_r.at[t])
        arrived(lead_g.at[x, behind], zg_r.at[t])
    total(1, second)
    deliver(1)
    share(0)
    share(1)
    for t in range(1, 4):
        there = (d, lax.rem(x + t, NX) * NZ + z)
        send(lead_b.at[x], lead_b.at[x], xb_s.at[t], xb_r.at[t], there).start()
        send(lead_g.at[x], lead_g.at[x], xg_s.at[t], xg_r.at[t], there).start()

    rows = lax.broadcasted_iota(jnp.int32, (256, 256), 0)
    cols = lax.broadcasted_iota(jnp.int32, (256, 256), 1)
    for side, (diag, border) in enumerate(factors):
        for j in range(16):
            mine_too = jnp.logical_or(from_j[0] == j, from_j[1] == j)

            @pl.when(jnp.logical_not(mine_too))
            def _():
                arrived(st.at[side, j], de_r.at[side, j])

        a = st[side, :, 0].reshape(256, 256)
        cross = st[side, :, 1].reshape(256, 256)
        lead = st[side, :, 2].reshape(256, 256)
        diag16, border16 = diag.astype(bf16), border.astype(bf16)
        u = dot16(cross, diag16) + dot16(lead, border16)
        v = dot16(a, diag16) + dot16(cross.T, border16)
        h = dot(diag16.astype(f32).T, v) + dot(border16.astype(f32).T, u)
        u_out[side] = u
        h_out[side] = h
        tr_h = jnp.sum(jnp.where(rows == cols, h, 0.0))
        tr_g = jnp.sum(diag * diag) + jnp.sum(border * border)
        tr[f, side * 2 : side * 2 + 1, :] = jnp.full((1, 128), tr_h, f32)
        tr[f, side * 2 + 1 : side * 2 + 2, :] = jnp.full((1, 128), tr_g, f32)
    tr[f, 4:8, :] = jnp.zeros((4, 128), f32)

    @pl.loop(1, 32)
    def _(t):
        send(tr.at[f], tr.at[f], tr_s.at[t], tr_r.at[t], (d, lax.rem(f + t, 32))).start()

    for t in range(1, 4):
        there = (d, lax.rem(x + t, NX) * NZ + z)
        behind = lax.rem(x + NX - t, NX)
        send(lead_b.at[x], lead_b.at[x], xb_s.at[t], xb_r.at[t], there).wait_send()
        send(lead_g.at[x], lead_g.at[x], xg_s.at[t], xg_r.at[t], there).wait_send()
        arrived(lead_b.at[behind], xb_r.at[t])
        arrived(lead_g.at[behind], xg_r.at[t])
    b0_out[...] = lead_b[...].reshape(512, 256)
    g0_out[...] = lead_g[...].reshape(1024, 256)
    for side in range(2):
        for m in range(2):
            there = (to_d, mine + 16 * m)

            @pl.when(jnp.logical_not(is_me(there)))
            def _():
                send(sm.at[side, m], st.at[side, slot], de_s.at[side, m], de_r.at[side, slot], there).wait_send()

        for i in range(2):
            j = from_j[i]
            for t in range(1, 8):
                there = (lax.rem(d + t, 8), f)
                send(st.at[side, j], st.at[side, j], ag_s.at[side, i, t], de_r.at[side, j], there).wait_send()

    @pl.loop(1, 32)
    def _(t):
        send(tr.at[f], tr.at[f], tr_s.at[t], tr_r.at[t], (d, lax.rem(f + t, 32))).wait_send()
        arrived(tr.at[lax.rem(f + 32 - t, 32)], tr_r.at[t])

    sums = tr[0]
    for i in range(1, 32):
        sums = sums + tr[i]
    tr_out[...] = sums


def advance_body(
    counts, traces, h_in, u_in, gram_in, k_factor, c_factor, k_moment, c_moment, leads,
    k_new, c_new, km_new, cm_new, k_half, c_half,
):
    f = lax.axis_index("fsdp")
    flag = jnp.where(f > 0, 1.0, 0.0)
    tokens = counts[0]
    for i in range(1, 8):
        tokens = tokens + counts[i]
    inverse = 1.0 / jnp.full((1, 1), tokens.astype(f32), f32)
    width = 8192.0
    trace = [traces[i : i + 1, 0:1] for i in range(4)]
    rows = lax.broadcasted_iota(jnp.int32, (256, 256), 0)
    cols = lax.broadcasted_iota(jnp.int32, (256, 256), 1)
    identity = jnp.where(rows == cols, 1.0, 0.0)
    for side, (factor, moment, f_new, m_new, half) in enumerate(
        ((k_factor, k_moment, k_new, km_new, k_half), (c_factor, c_moment, c_new, cm_new, c_half))
    ):
        other_h = trace[2 - 2 * side] * inverse * inverse
        other_g = trace[3 - 2 * side] * damping
        diag = factor[0, :, 0:256]
        border = factor[0, :, 256:512] * flag
        lead = leads[side * 256 : side * 256 + 256, :].astype(f32)
        fresh = (other_h * h_in[side] + other_g * gram_in[side] - width * identity) / (2.0 * width)
        cross = dot(lead.T, other_h * u_in[side] + other_g * border) * flag / (2.0 * width)
        m_diag = momentum_rate * moment[0, :, 0:256] + fresh
        m_side = (momentum_rate * moment[0, :, 256:512] + cross) * flag
        n_diag = diag - step_rate * dot(diag, m_diag)
        n_side = (border - step_rate * (dot(lead, m_side) + dot(border, m_diag))) * flag
        f_new[0, :, 0:256] = n_diag
        f_new[0, :, 256:512] = n_side
        m_new[0, :, 0:256] = m_diag
        m_new[0, :, 256:512] = m_side
        half[0:256, :] = n_diag.astype(bf16)
        half[256:512, :] = n_side.astype(bf16)


def precond_body(
    k_half, c_half, grad, grad_lead, out,
    lead_src, lead_in, own, lead_sum, all_lead, second, lead_rows, cb, term, terms, part,
    rs_s, rs_r, ga_s, ga_r, ca_s, ca_r, cz_s, cz_r, cx_s, cx_r, ro_s, ro_r, te_s, te_r,
):
    x, y, z, c = position()
    d, f = lax.axis_index("dp"), lax.axis_index("fsdp")
    barrier = pltpu.get_barrier_semaphore()

    @pl.loop(1, 32)
    def _(t):
        greet(barrier, (d, lax.rem(f + t, 32)))

    @pl.when(d == 0)
    def _():
        for t in range(1, 8):
            greet(barrier, (t, f))

    @pl.when(d > 0)
    def _():
        greet(barrier, (0, f))

    k_diag, k_side = k_half[0:256, :], k_half[256:512, :]
    first = (dot16(grad[...], k_diag) + dot16(grad_lead[...], k_side)).astype(bf16)
    lead_src[...] = dot16(first, k_side.T).astype(bf16).reshape(32, 32, 256)
    pl.semaphore_wait(barrier, 31 + jnp.where(d == 0, 7, 1))

    holder = lax.div(z, 4) == c
    root = jnp.logical_and(holder, x == y)
    j = lax.rem(z, 4)

    def quarter(t):
        return c_half.at[pl.ds(pl.multiple_of(t * 128, 128), 128)]

    def scatter_copy(t):
        to = lax.rem(x + t, NX)
        return send(quarter(to), cb.at[to, j], ca_s.at[t], ca_r, (d, to * NZ + z))

    @pl.when(root)
    def _():
        for t in range(1, 4):
            scatter_copy(t).start()
        pltpu.make_async_copy(quarter(x), cb.at[x, j], ca_r).start()

    own_piece = pltpu.make_async_copy(lead_src.at[f], lead_in.at[f], rs_r.at[0])
    own_piece.start()

    @pl.loop(1, 32)
    def _(t):
        there = lax.rem(f + t, 32)
        send(lead_src.at[there], lead_in.at[f], rs_s.at[t], rs_r.at[t], (d, there)).start()

    own[...] = dot16(first, k_diag.T)

    def ring_copy(t):
        return send(cb.at[x, j], cb.at[x, j], cz_s.at[t], cz_r.at[j], (d, x * NZ + lax.rem(z + t, NZ)))

    @pl.when(holder)
    def _():
        arrived(cb.at[x, j], ca_r)
        for t in range(1, 8):
            ring_copy(t).start()

    own_piece.wait()

    @pl.loop(1, 32)
    def _(t):
        there = lax.rem(f + t, 32)
        send(lead_src.at[there], lead_in.at[f], rs_s.at[t], rs_r.at[t], (d, there)).wait_send()
        arrived(lead_in.at[lax.rem(f + 32 - t, 32)], rs_r.at[t])

    total = lead_in[0].astype(f32)
    for i in range(1, 32):
        total = total + lead_in[i].astype(f32)
    lead_sum[...] = total.astype(bf16)
    second[...] = own[...].astype(bf16)

    @pl.when(f > 0)
    def _():
        send(lead_sum, all_lead.at[f], ga_s, ga_r.at[f], (d, 0)).start()

    for i in range(4):

        @pl.when(jnp.logical_or(jnp.logical_not(holder), j != i))
        def _():
            arrived(cb.at[x, i], cz_r.at[i])

    def spread_copy(t):
        return send(cb.at[x], cb.at[x], cx_s.at[t], cx_r.at[t], (d, lax.rem(x + t, NX) * NZ + z))

    for t in range(1, 4):
        spread_copy(t).start()

    @pl.when(f == 0)
    def _():
        all_lead[0] = lead_sum[...]
        for i in range(1, 32):
            arrived(all_lead.at[i], ga_r.at[i])
        second[...] = (own[...] + all_lead[...].reshape(1024, 256).astype(f32)).astype(bf16)

    src = second.at[0:256]

    @pl.when(d == 0)
    def _():
        for t in range(1, 8):
            send(src, lead_rows, ro_s.at[t], ro_r, (t, f)).start()
        pltpu.make_async_copy(src, lead_rows, ro_r).start()

    for t in range(1, 4):
        arrived(cb.at[lax.rem(x + NX - t, NX)], cx_r.at[t])
    for i in range(4):
        diag = cb[0:2, i].reshape(256, 256)
        part[i] = dot16(diag.T, second[i * 256 : i * 256 + 256, :])
    arrived(lead_rows, ro_r)
    sum_term = jnp.zeros((256, 256), f32)
    for i in range(4):
        diag = cb[0:2, i].reshape(256, 256)
        side = cb[2:4, i].reshape(256, 256)
        third = (part[i] + dot16(side.T, lead_rows[...])).astype(bf16)
        own[i * 256 : i * 256 + 256, :] = dot16(diag, third)
        sum_term = sum_term + dot16(side, third)
    term[...] = sum_term.astype(bf16)

    @pl.when(d > 0)
    def _():
        send(term, terms.at[d], te_s, te_r.at[d], (0, f)).start()

    out[256:1024, :] = own[256:1024, :].astype(bf16)

    @pl.when(d > 0)
    def _():
        out[0:256, :] = own[0:256, :].astype(bf16)
        send(term, terms.at[d], te_s, te_r.at[d], (0, f)).wait_send()

    @pl.when(d == 0)
    def _():
        whole = own[0:256, :] + sum_term
        for t in range(1, 8):
            arrived(terms.at[t], te_r.at[t])
            whole = whole + terms[t].astype(f32)
        out[0:256, :] = whole.astype(bf16)
        for t in range(1, 8):
            send(src, lead_rows, ro_s.at[t], ro_r, (t, f)).wait_send()

    @pl.when(root)
    def _():
        for t in range(1, 4):
            scatter_copy(t).wait_send()

    @pl.when(holder)
    def _():
        for t in range(1, 8):
            ring_copy(t).wait_send()

    for t in range(1, 4):
        spread_copy(t).wait_send()

    @pl.when(f > 0)
    def _():
        send(lead_sum, all_lead.at[f], ga_s, ga_r.at[f], (d, 0)).wait_send()


def per_device(acts, out_grads, token_counts, k_factor, c_factor, k_moment, c_moment, grad_weight):
    SM = pl.BlockSpec(memory_space=pltpu.SMEM)
    V = pltpu.VMEM
    xc, x0, piece_b, piece_g = call(
        token_body, "tokens", (token_counts, acts, out_grads, k_factor, c_factor, grad_weight), [SM] + [VM] * 5,
        [((2, 32, 64, 512), bf16), ((2, 32, 64, 256), bf16), ((16, 256), bf16), ((32, 256), bf16)], [ANY] * 4,
        [V((16, 2, 2, 64, 512), bf16), V((2, 2, 2, 64, 128), bf16), V((512, 256), bf16)]
        + [DMA((32,))] * 5 + [DMA((2,)), DMA((2,)), DMA((32,)), DMA((32,)), DMA((32,))],
        0,
    )
    h, u, grams, traces, leads, grad_lead = call(
        stats_body, "stats",
        (xc.reshape(2, 2048, 512), x0.reshape(2, 2048, 256), k_factor, c_factor, piece_b, piece_g),
        [VM] * 4 + [ANY] * 2,
        [((2, 256, 256), f32)] * 3 + [((8, 128), f32), ((512, 256), bf16), ((1024, 256), bf16)], [VM] * 6,
        [V((2, 16, 5, 16, 256), bf16), V((2, 16, 5, 16, 256), bf16), V((2, 2, 3, 16, 256), bf16),
         V((2, 16, 3, 16, 256), bf16), V((32, 8, 128), f32), V((4, 8, 16, 256), bf16), V((4, 8, 32, 256), bf16),
         DMA((2, 16)), DMA((2, 16)), DMA((2, 2)), DMA((2, 16)), DMA((2, 2, 8)), DMA((8,)), DMA((8,)), DMA((8,)),
         DMA((8,)), DMA((4,)), DMA((4,)), DMA((4,)), DMA((4,)), DMA((32,)), DMA((32,))],
        1,
    )
    k_new, c_new, km_new, cm_new, k_half, c_half = call(
        advance_body, "advance",
        (token_counts, traces, h, u, grams, k_factor, c_factor, k_moment, c_moment, leads), [SM] + [VM] * 9,
        [((1, 256, 512), f32)] * 4 + [((512, 256), bf16)] * 2, [VM] * 6,
    )
    (precond,) = call(
        precond_body, "precond", (k_half, c_half, grad_weight, grad_lead), [VM] * 4, [((1024, 256), bf16)], [VM],
        [V((32, 32, 256), bf16), V((32, 32, 256), bf16), V((1024, 256), f32), V((32, 256), bf16),
         V((32, 32, 256), bf16), V((1024, 256), bf16), V((256, 256), bf16), V((4, 4, 128, 256), bf16),
         V((256, 256), bf16), V((8, 256, 256), bf16), V((4, 256, 256), f32),
         DMA((32,)), DMA((32,)), DMA, DMA((32,)), DMA((4,)), DMA, DMA((8,)), DMA((4,)), DMA((4,)), DMA((4,)),
         DMA((8,)), DMA, DMA, DMA((8,))],
        2,
    )
    return k_new, c_new, km_new, cm_new, precond


def solution(mesh):
    in_specs = (
        P(("dp", "fsdp"), None),
        P(("dp", "fsdp"), None),
        P(),
        P("fsdp", None, None),
        P("fsdp", None, None),
        P("fsdp", None, None),
        P("fsdp", None, None),
        P("dp", "fsdp"),
    )
    out_specs = (
        P("fsdp", None, None),
        P("fsdp", None, None),
        P("fsdp", None, None),
        P("fsdp", None, None),
        P("dp", "fsdp"),
    )
    return jax.shard_map(per_device, mesh=mesh, in_specs=in_specs, out_specs=out_specs, check_vma=False)
```

```python
import functools

import jax
import jax.numpy as jnp
from jax import lax
from jax.experimental import pallas as pl
from jax.experimental.pallas import tpu as pltpu
from jax.sharding import PartitionSpec as P

MESH = pl.DeviceIdType.MESH
highest = lax.Precision.HIGHEST
f32 = jnp.float32
bf16 = jnp.bfloat16

damping = 0.1
momentum_rate = 0.5
step_rate = 0.2

NX, NY, NZ = 4, 4, 8


def position():
    d = lax.axis_index("dp")
    f = lax.axis_index("fsdp")
    return lax.div(f, NZ), lax.div(d, 2), lax.rem(f, NZ), lax.rem(d, 2)


def device(x, y, z, c):
    return (y * 2 + c, x * NZ + z)


def class_of(x, y, z, c):
    return lax.rem(x, 2) * 8 + lax.rem(y, 2) * 4 + c * 2 + lax.rem(z, 2)


def send(src, dst, send_sem, recv_sem, target):
    return pltpu.make_async_remote_copy(
        src_ref=src, dst_ref=dst, send_sem=send_sem, recv_sem=recv_sem, device_id=target, device_id_type=MESH
    )


def arrived(dst, sem):
    pltpu.make_async_copy(dst, dst, sem).wait()


def greet(barrier, target):
    pl.semaphore_signal(barrier, inc=1, device_id=target, device_id_type=MESH)


ANY = pl.BlockSpec(memory_space=pl.ANY)
VM = pl.BlockSpec(memory_space=pltpu.VMEM)
DMA = pltpu.SemaphoreType.DMA


def call(body, name, ins, in_specs, outs, out_specs, scratch=(), cid=None):
    params = dict(collective_id=cid, has_side_effects=True) if cid is not None else {}
    return pl.pallas_call(
        body,
        out_shape=[jax.ShapeDtypeStruct(s, t) for s, t in outs],
        in_specs=in_specs,
        out_specs=out_specs,
        scratch_shapes=list(scratch),
        compiler_params=pltpu.CompilerParams(**params),
        name=name,
    )(*ins)


def dot(a, b):
    return jnp.dot(a, b, precision=highest, preferred_element_type=f32)


def dot16(a, b):
    return jnp.dot(a, b, preferred_element_type=f32)


def stats_body(
    counts, acts, grads, k_factor, c_factor, grad, h_out, u_out, gram_out, tr_out, b0_out, g0_out,
    raw, xs, ls, xc, x0, b0, piece_b, piece_g, ps, pi, sm, st, tr, lead_b, lead_g,
    in_s, s1, r1, s2, r2, s5, r4, s3, s4, r3,
    rs_s, rs_r, de_s, de_r, a0_s, a0_r, ag_s, fw_s, zb_s, zb_r, zg_s, zg_r, xb_s, xb_r, xg_s, xg_r, tr_s, tr_r,
):
    x, y, z, c = position()
    d, f = lax.axis_index("dp"), lax.axis_index("fsdp")
    barrier = pltpu.get_barrier_semaphore()
    loads = [pltpu.make_async_copy(ref, raw.at[i], in_s.at[i]) for i, ref in enumerate((acts, grads))]
    for one in loads:
        one.start()
    partner = device(x, y, z, 1 - c)

    def cell(sign, a, b, g, e):
        return (
            lax.rem(x + sign * a + NX, NX),
            lax.rem(y + sign * b + NY, NY),
            lax.rem(z + sign * g + NZ, NZ),
            lax.rem(c + e, 2),
        )

    offsets = [(a, b, g, e) for a in (0, 1) for b in (0, 1) for g in (0, 1) for e in (0, 1)]
    mine = class_of(x, y, z, c)
    xi, yi, zi = lax.div(x, 2), lax.div(y, 2), lax.div(z, 2)
    slot = xi * 8 + yi * 4 + zi
    mates = [(a, b, g) for a in range(2) for b in range(2) for g in range(4)]

    def mate(a, b, g):
        return lax.rem(x + 2 * a, NX), lax.rem(y + 2 * b, NY), lax.rem(z + 2 * g, NZ)

    k = lax.rem(f, 16)
    px, py, pc, pz = lax.div(k, 8), lax.rem(lax.div(k, 4), 2), lax.rem(lax.div(k, 2), 2), lax.rem(k, 2)

    def group_for(parity):
        return lax.rem(2 * yi + parity + lax.rem(zi, 2), NY) * 2 + lax.div(zi, 2)

    def slots_at(there_y):
        shift = lax.rem(there_y + py, 2)
        low = lax.div(lax.rem(there_y - shift + NY, NY), 2) * 4 + 2 * c + shift
        return [low, low + 8]

    def owner(j, qx, qy, qz, qc):
        return device(qx + 2 * lax.div(j, 8), qy + 2 * lax.rem(lax.div(j, 4), 2), qz + 2 * lax.rem(j, 4), qc)

    to_d = group_for(lax.rem(y, 2))
    from_j = slots_at(y)

    def is_me(there):
        return jnp.logical_and(there[0] == d, there[1] == f)

    def lead_target(t):
        return (group_for(lax.rem(lax.div(t, 4), 2)), t)

    for sign in (1, -1):
        for o in offsets:
            if o[:3] == (0, 0, 0) and (o[3] == 0 or sign == -1):
                continue
            greet(barrier, device(*cell(sign, *o)))
    for o in mates[1:]:
        greet(barrier, device(*mate(*o), c))

    @pl.loop(1, 32)
    def _(t):
        greet(barrier, (d, lax.rem(f + t, 32)))

    for t in range(1, 4):
        greet(barrier, device(x, lax.rem(y + t, NY), z, c))
    for j in from_j:
        for there in (owner(j, px, py, pz, pc), owner(j, 0, 0, 0, 0)):

            @pl.when(jnp.logical_not(is_me(there)))
            def _():
                greet(barrier, there)

    limit = counts[0] * jnp.where(d == 0, 1, 0)
    for i in range(1, 8):
        limit = limit + counts[i] * jnp.where(d == i, 1, 0)
    kept = []
    for h in range(2):
        at_slot = lax.broadcasted_iota(jnp.int32, (64, 256), 0) + (f * 128 + h * 64)
        kept.append(jnp.where(at_slot < limit, 1.0, 0.0).astype(bf16))

    def mask(side):
        loads[side].wait()
        for h in range(2):
            rows = slice(h * 64, h * 64 + 64)
            lead = raw[side, rows, 0:256] * kept[h]
            ls[side, 0, h, :, :] = lead[:, 0:128]
            ls[side, 1, h, :, :] = lead[:, 128:256]
            for i in range(16):
                for m in range(2):
                    n = m * 16 + i
                    cols = slice(m * 256, m * 256 + 256)
                    xs[side, i, h, :, cols] = raw[side, rows, n * 256 : n * 256 + 256] * kept[h]

    half = pl.ds(pl.multiple_of(c * 128, 128), 128)
    other_half = pl.ds(pl.multiple_of(128 - c * 128, 128), 128)

    def exchange(side):
        copies = []
        for i in (14, 15, 12, 13, 10, 11, 6, 7, 8, 9, 4, 5, 2, 3, 1, 0):
            for h, sign in ((0, 1), (1, -1)):
                there = cell(sign, *offsets[i])
                to = class_of(*there)
                at = h * 16 + i
                if i == 0:
                    one = pltpu.make_async_copy(xs.at[side, to, h], xc.at[side, at], r1.at[side, at])
                    two = pltpu.make_async_copy(ls.at[side, c, h], x0.at[side, at, :, half], r2.at[side, at])
                else:
                    tc = there[3]
                    to_half = pl.ds(pl.multiple_of(tc * 128, 128), 128)
                    dst = device(*there)
                    one = send(xs.at[side, to, h], xc.at[side, at], s1.at[side, at], r1.at[side, at], dst)
                    two = send(ls.at[side, tc, h], x0.at[side, at, :, to_half], s2.at[side, at], r2.at[side, at], dst)
                two.start()
                one.start()
                copies.append((i, at, one, two))
        return copies

    def collect(side, copies):
        passed = []
        for i, at, one, two in copies:
            got = x0.at[side, at, :, half]
            arrived(got, r2.at[side, at])
            on = send(got, x0.at[side, at ^ 1, :, half], s5.at[side, at], r4.at[side, at ^ 1], partner)
            on.start()
            passed.append(on)
        for i, at, one, two in copies:
            arrived(xc.at[side, at], r1.at[side, at])
        for i, at, one, two in copies:
            arrived(x0.at[side, at, :, other_half], r4.at[side, at])
        return passed

    def grad_piece(t):
        return grad.at[pl.ds(pl.multiple_of(t * 32, 32), 32)]

    def lead_piece(t):
        return b0.at[pl.ds(pl.multiple_of(t * 16, 16), 16)]

    @pl.when(f == 0)
    def _():
        b0[0:256, :] = k_factor[0, :, 0:256].astype(bf16)
        b0[256:512, :] = c_factor[0, :, 0:256].astype(bf16)

    mask(0)
    to_self = jnp.where(is_me((to_d, mine)), 1, 0) + jnp.where(is_me((to_d, mine + 16)), 1, 0)
    lead_self = jnp.where(is_me(lead_target(f)), 1, 0)
    pl.semaphore_wait(barrier, 29 + 15 + 31 + 3 + 2 - to_self + jnp.where(mine == 0, 32 - lead_self, 0))
    tokens = [exchange(0)]
    mask(1)
    tokens.append(exchange(1))

    @pl.when(f == 0)
    def _():
        pltpu.make_async_copy(grad_piece(0), piece_g, r3.at[0]).start()
        pltpu.make_async_copy(lead_piece(0), piece_b, r3.at[1]).start()

        @pl.loop(1, 32)
        def _(t):
            send(grad_piece(t), piece_g, s3.at[t], r3.at[0], (d, t)).start()
            send(lead_piece(t), piece_b, s4.at[t], r3.at[1], (d, t)).start()

    flag = jnp.where(f > 0, 1.0, 0.0)
    for side, factor in enumerate((k_factor, c_factor)):
        diag = factor[0, :, 0:256]
        border = factor[0, :, 256:512] * flag
        gram_out[side] = dot(diag.T, diag) + dot(border.T, border)
        tr_g = jnp.sum(diag * diag) + jnp.sum(border * border)
        tr[f, side * 2 + 1 : side * 2 + 2, :] = jnp.full((1, 128), tr_g, f32)
    tr[f, 4:8, :] = jnp.zeros((4, 128), f32)

    dims = (((0,), (0,)), ((), ()))

    def gram(side):
        lead = x0[side].reshape(2048, 256)
        a = xc[side, :, :, 0:256].reshape(2048, 256)
        b = xc[side, :, :, 256:512].reshape(2048, 256)
        for i, (left, right) in enumerate(((a, a), (b, b), (lead, a), (lead, b))):
            g = lax.dot_general(left, right, dims, preferred_element_type=f32)
            ps[side, :, i, :, :] = g.astype(bf16).reshape(16, 16, 256)

    def scatter(side):
        copies = []
        for i, o in enumerate(mates):
            if i > 0:
                tx, ty, tz = mate(*o)
                j = lax.div(tx, 2) * 8 + lax.div(ty, 2) * 4 + lax.div(tz, 2)
                copy = send(ps.at[side, j], pi.at[side, i], rs_s.at[side, i], rs_r.at[side, i], device(tx, ty, tz, c))
                copy.start()
                copies.append(copy)
        return copies

    passed = collect(0, tokens[0])
    gram(0)
    sums = [scatter(0)]
    passed += collect(1, tokens[1])
    gram(1)
    sums.append(scatter(1))

    arrived(piece_g, r3.at[0])
    arrived(piece_b, r3.at[1])
    own_b = pltpu.make_async_copy(piece_b, lead_b.at[x, z], zb_r.at[0])
    own_g = pltpu.make_async_copy(piece_g, lead_g.at[x, z], zg_r.at[0])
    own_b.start()
    own_g.start()
    for t in range(1, 8):
        there = (d, x * NZ + lax.rem(z + t, NZ))
        send(piece_b, lead_b.at[x, z], zb_s.at[t], zb_r.at[t], there).start()
        send(piece_g, lead_g.at[x, z], zg_s.at[t], zg_r.at[t], there).start()

    def total(side):
        for copy in sums[side]:
            copy.wait()
        value = ps[side, slot].astype(f32)
        for i in range(1, 16):
            value = value + pi[side, i].astype(f32)
        value = value.astype(bf16)
        for m in range(2):
            for q in range(2):
                sm[side, m, q] = value[2 * q + m]

    def lead_send(side, t):
        return send(sm.at[side, 0, 0], st.at[side, slot, 2], a0_s.at[side, t], a0_r.at[side, slot], lead_target(t))

    def rows_send(side, m):
        there = (to_d, mine + 16 * m)
        return send(sm.at[side, m], st.at[side, slot, 0:2], de_s.at[side, m], de_r.at[side, slot], there)

    def deliver(side):
        @pl.when(mine == 0)
        def _():
            @pl.loop(0, 32)
            def _(t):
                me = is_me(lead_target(t))

                @pl.when(me)
                def _():
                    pltpu.make_async_copy(sm.at[side, 0, 0], st.at[side, slot, 2], a0_r.at[side, slot]).start()

                @pl.when(jnp.logical_not(me))
                def _():
                    lead_send(side, t).start()

        for m in range(2):
            me = is_me((to_d, mine + 16 * m))

            @pl.when(me)
            def _():
                pltpu.make_async_copy(sm.at[side, m], st.at[side, slot, 0:2], de_r.at[side, slot]).start()

            @pl.when(jnp.logical_not(me))
            def _():
                rows_send(side, m).start()

    def share_send(side, i, t):
        there = device(x, lax.rem(y + t, NY), z, c) if t > 0 else partner
        at = st.at[side, from_j[i]]
        return send(at, at, ag_s.at[side, i, t], de_r.at[side, from_j[i]], there)

    def pass_send(side, i, t):
        j = slots_at(lax.rem(y + NY - t, NY))[i]
        return send(st.at[side, j], st.at[side, j], fw_s.at[side, i, t], de_r.at[side, j], partner)

    def share(side):
        for i in range(2):
            arrived(st.at[side, from_j[i], 0:2], de_r.at[side, from_j[i]])
            arrived(st.at[side, from_j[i], 2], a0_r.at[side, from_j[i]])
            for t in (1, 2, 3, 0):
                share_send(side, i, t).start()

    def pass_on(side):
        for t in (1, 3, 2):
            for i in range(2):
                j = slots_at(lax.rem(y + NY - t, NY))[i]
                arrived(st.at[side, j], de_r.at[side, j])
                pass_send(side, i, t).start()

    total(0)
    deliver(0)
    own_b.wait()
    own_g.wait()
    for t in range(1, 8):
        there = (d, x * NZ + lax.rem(z + t, NZ))
        behind = lax.rem(z + NZ - t, NZ)
        send(piece_b, lead_b.at[x, z], zb_s.at[t], zb_r.at[t], there).wait_send()
        send(piece_g, lead_g.at[x, z], zg_s.at[t], zg_r.at[t], there).wait_send()
        arrived(lead_b.at[x, behind], zb_r.at[t])
        arrived(lead_g.at[x, behind], zg_r.at[t])
    share(0)
    total(1)
    deliver(1)
    pass_on(0)
    share(1)
    for t in range(1, 4):
        there = (d, lax.rem(x + t, NX) * NZ + z)
        send(lead_b.at[x], lead_b.at[x], xb_s.at[t], xb_r.at[t], there).start()
        send(lead_g.at[x], lead_g.at[x], xg_s.at[t], xg_r.at[t], there).start()

    rows = lax.broadcasted_iota(jnp.int32, (256, 256), 0)
    cols = lax.broadcasted_iota(jnp.int32, (256, 256), 1)

    def second_moment(side):
        for j in range(16):
            @pl.when(lax.div(j % 4, 2) != c)
            def _():
                arrived(st.at[side, j], de_r.at[side, j])

        factor = (k_factor, c_factor)[side]
        diag16 = factor[0, :, 0:256].astype(bf16)
        border16 = (factor[0, :, 256:512] * flag).astype(bf16)
        a = st[side, :, 0].reshape(256, 256)
        cross = st[side, :, 1].reshape(256, 256)
        lead = st[side, :, 2].reshape(256, 256)
        u = dot16(cross, diag16) + dot16(lead, border16)
        v = dot16(a, diag16) + dot16(cross.T, border16)
        h = dot(diag16.astype(f32).T, v) + dot(border16.astype(f32).T, u)
        u_out[side] = u
        h_out[side] = h
        tr[f, side * 2 : side * 2 + 1, :] = jnp.full((1, 128), jnp.sum(jnp.where(rows == cols, h, 0.0)), f32)

    second_moment(0)
    pass_on(1)
    second_moment(1)

    @pl.loop(1, 32)
    def _(t):
        send(tr.at[f], tr.at[f], tr_s.at[t], tr_r.at[t], (d, lax.rem(f + t, 32))).start()

    for t in range(1, 4):
        there = (d, lax.rem(x + t, NX) * NZ + z)
        behind = lax.rem(x + NX - t, NX)
        send(lead_b.at[x], lead_b.at[x], xb_s.at[t], xb_r.at[t], there).wait_send()
        send(lead_g.at[x], lead_g.at[x], xg_s.at[t], xg_r.at[t], there).wait_send()
        arrived(lead_b.at[behind], xb_r.at[t])
        arrived(lead_g.at[behind], xg_r.at[t])
    b0_out[...] = lead_b[...].reshape(512, 256)
    g0_out[...] = lead_g[...].reshape(1024, 256)
    for on in passed:
        on.wait_send()
    for copies in tokens:
        for i, at, one, two in copies:
            if i > 0:
                one.wait_send()
                two.wait_send()

    @pl.when(f == 0)
    def _():
        @pl.loop(1, 32)
        def _(t):
            send(grad_piece(t), piece_g, s3.at[t], r3.at[0], (d, t)).wait_send()
            send(lead_piece(t), piece_b, s4.at[t], r3.at[1], (d, t)).wait_send()

    for side in range(2):

        @pl.when(mine == 0)
        def _():
            @pl.loop(0, 32)
            def _(t):
                @pl.when(jnp.logical_not(is_me(lead_target(t))))
                def _():
                    lead_send(side, t).wait_send()

        for m in range(2):

            @pl.when(jnp.logical_not(is_me((to_d, mine + 16 * m))))
            def _():
                rows_send(side, m).wait_send()

        for i in range(2):
            for t in range(4):
                share_send(side, i, t).wait_send()
            for t in range(1, 4):
                pass_send(side, i, t).wait_send()

    @pl.loop(1, 32)
    def _(t):
        send(tr.at[f], tr.at[f], tr_s.at[t], tr_r.at[t], (d, lax.rem(f + t, 32))).wait_send()
        arrived(tr.at[lax.rem(f + 32 - t, 32)], tr_r.at[t])

    result = tr[0]
    for i in range(1, 32):
        result = result + tr[i]
    tr_out[...] = result


def advance_body(
    counts, traces, h_in, u_in, gram_in, k_factor, c_factor, k_moment, c_moment, leads,
    k_new, c_new, km_new, cm_new, k_half, c_half,
):
    f = lax.axis_index("fsdp")
    flag = jnp.where(f > 0, 1.0, 0.0)
    tokens = counts[0]
    for i in range(1, 8):
        tokens = tokens + counts[i]
    inverse = 1.0 / jnp.full((1, 1), tokens.astype(f32), f32)
    width = 8192.0
    trace = [traces[i : i + 1, 0:1] for i in range(4)]
    rows = lax.broadcasted_iota(jnp.int32, (256, 256), 0)
    cols = lax.broadcasted_iota(jnp.int32, (256, 256), 1)
    identity = jnp.where(rows == cols, 1.0, 0.0)
    for side, (factor, moment, f_new, m_new, half) in enumerate(
        ((k_factor, k_moment, k_new, km_new, k_half), (c_factor, c_moment, c_new, cm_new, c_half))
    ):
        other_h = trace[2 - 2 * side] * inverse * inverse
        other_g = trace[3 - 2 * side] * damping
        diag = factor[0, :, 0:256]
        border = factor[0, :, 256:512] * flag
        lead = leads[side * 256 : side * 256 + 256, :].astype(f32)
        fresh = (other_h * h_in[side] + other_g * gram_in[side] - width * identity) / (2.0 * width)
        cross = dot(lead.T, other_h * u_in[side] + other_g * border) * flag / (2.0 * width)
        m_diag = momentum_rate * moment[0, :, 0:256] + fresh
        m_side = (momentum_rate * moment[0, :, 256:512] + cross) * flag
        n_diag = diag - step_rate * dot(diag, m_diag)
        n_side = (border - step_rate * (dot(lead, m_side) + dot(border, m_diag))) * flag
        f_new[0, :, 0:256] = n_diag
        f_new[0, :, 256:512] = n_side
        m_new[0, :, 0:256] = m_diag
        m_new[0, :, 256:512] = m_side
        half[0:256, :] = n_diag.astype(bf16)
        half[256:512, :] = n_side.astype(bf16)


def precond_body(
    k_half, c_half, grad, grad_lead, out,
    lead_src, lead_in, own, lead_sum, all_lead, second, lead_rows, cb, term, terms, part,
    rs_s, rs_r, ga_s, ga_r, ca_s, ca_r, cz_s, cz_r, cx_s, cx_r, ro_s, ro_r, te_s, te_r,
):
    x, y, z, c = position()
    d, f = lax.axis_index("dp"), lax.axis_index("fsdp")
    barrier = pltpu.get_barrier_semaphore()

    @pl.loop(1, 32)
    def _(t):
        greet(barrier, (d, lax.rem(f + t, 32)))

    @pl.when(d == 0)
    def _():
        for t in range(1, 8):
            greet(barrier, (t, f))

    @pl.when(d > 0)
    def _():
        greet(barrier, (0, f))

    k_diag, k_side = k_half[0:256, :], k_half[256:512, :]
    first = (dot16(grad[...], k_diag) + dot16(grad_lead[...], k_side)).astype(bf16)
    lead_src[...] = dot16(first, k_side.T).astype(bf16).reshape(32, 32, 256)
    pl.semaphore_wait(barrier, 31 + jnp.where(d == 0, 7, 1))

    holder = lax.div(z, 4) == c
    root = jnp.logical_and(holder, x == y)
    j = lax.rem(z, 4)

    def quarter(t):
        return c_half.at[pl.ds(pl.multiple_of(t * 128, 128), 128)]

    def scatter_copy(t):
        to = lax.rem(x + t, NX)
        return send(quarter(to), cb.at[to, j], ca_s.at[t], ca_r, (d, to * NZ + z))

    @pl.when(root)
    def _():
        for t in range(1, 4):
            scatter_copy(t).start()
        pltpu.make_async_copy(quarter(x), cb.at[x, j], ca_r).start()

    own_piece = pltpu.make_async_copy(lead_src.at[f], lead_in.at[f], rs_r.at[0])
    own_piece.start()

    @pl.loop(1, 32)
    def _(t):
        there = lax.rem(f + t, 32)
        send(lead_src.at[there], lead_in.at[f], rs_s.at[t], rs_r.at[t], (d, there)).start()

    own[...] = dot16(first, k_diag.T)

    def ring_copy(t):
        return send(cb.at[x, j], cb.at[x, j], cz_s.at[t], cz_r.at[j], (d, x * NZ + lax.rem(z + t, NZ)))

    @pl.when(holder)
    def _():
        arrived(cb.at[x, j], ca_r)
        for t in range(1, 8):
            ring_copy(t).start()

    own_piece.wait()

    @pl.loop(1, 32)
    def _(t):
        there = lax.rem(f + t, 32)
        send(lead_src.at[there], lead_in.at[f], rs_s.at[t], rs_r.at[t], (d, there)).wait_send()
        arrived(lead_in.at[lax.rem(f + 32 - t, 32)], rs_r.at[t])

    total = lead_in[0].astype(f32)
    for i in range(1, 32):
        total = total + lead_in[i].astype(f32)
    lead_sum[...] = total.astype(bf16)
    second[...] = own[...].astype(bf16)

    @pl.when(f > 0)
    def _():
        send(lead_sum, all_lead.at[f], ga_s, ga_r.at[f], (d, 0)).start()

    for i in range(4):

        @pl.when(jnp.logical_or(jnp.logical_not(holder), j != i))
        def _():
            arrived(cb.at[x, i], cz_r.at[i])

    def spread_copy(t):
        return send(cb.at[x], cb.at[x], cx_s.at[t], cx_r.at[t], (d, lax.rem(x + t, NX) * NZ + z))

    for t in range(1, 4):
        spread_copy(t).start()

    @pl.when(f == 0)
    def _():
        all_lead[0] = lead_sum[...]
        for i in range(1, 32):
            arrived(all_lead.at[i], ga_r.at[i])
        second[...] = (own[...] + all_lead[...].reshape(1024, 256).astype(f32)).astype(bf16)

    src = second.at[0:256]

    @pl.when(d == 0)
    def _():
        for t in range(1, 8):
            send(src, lead_rows, ro_s.at[t], ro_r, (t, f)).start()
        pltpu.make_async_copy(src, lead_rows, ro_r).start()

    for t in range(1, 4):
        arrived(cb.at[lax.rem(x + NX - t, NX)], cx_r.at[t])
    for i in range(4):
        diag = cb[0:2, i].reshape(256, 256)
        part[i] = dot16(diag.T, second[i * 256 : i * 256 + 256, :])
    arrived(lead_rows, ro_r)
    sum_term = jnp.zeros((256, 256), f32)
    for i in range(4):
        diag = cb[0:2, i].reshape(256, 256)
        side = cb[2:4, i].reshape(256, 256)
        third = (part[i] + dot16(side.T, lead_rows[...])).astype(bf16)
        own[i * 256 : i * 256 + 256, :] = dot16(diag, third)
        sum_term = sum_term + dot16(side, third)
    term[...] = sum_term.astype(bf16)

    @pl.when(d > 0)
    def _():
        send(term, terms.at[d], te_s, te_r.at[d], (0, f)).start()

    out[256:1024, :] = own[256:1024, :].astype(bf16)

    @pl.when(d > 0)
    def _():
        out[0:256, :] = own[0:256, :].astype(bf16)
        send(term, terms.at[d], te_s, te_r.at[d], (0, f)).wait_send()

    @pl.when(d == 0)
    def _():
        whole = own[0:256, :] + sum_term
        for t in range(1, 8):
            arrived(terms.at[t], te_r.at[t])
            whole = whole + terms[t].astype(f32)
        out[0:256, :] = whole.astype(bf16)
        for t in range(1, 8):
            send(src, lead_rows, ro_s.at[t], ro_r, (t, f)).wait_send()

    @pl.when(root)
    def _():
        for t in range(1, 4):
            scatter_copy(t).wait_send()

    @pl.when(holder)
    def _():
        for t in range(1, 8):
            ring_copy(t).wait_send()

    for t in range(1, 4):
        spread_copy(t).wait_send()

    @pl.when(f > 0)
    def _():
        send(lead_sum, all_lead.at[f], ga_s, ga_r.at[f], (d, 0)).wait_send()


def per_device(acts, out_grads, token_counts, k_factor, c_factor, k_moment, c_moment, grad_weight):
    SM = pl.BlockSpec(memory_space=pltpu.SMEM)
    V = pltpu.VMEM
    h, u, grams, traces, leads, grad_lead = call(
        stats_body, "stats",
        (token_counts, acts, out_grads, k_factor, c_factor, grad_weight), [SM, ANY, ANY, VM, VM, ANY],
        [((2, 256, 256), f32)] * 3 + [((8, 128), f32), ((512, 256), bf16), ((1024, 256), bf16)], [VM] * 6,
        [V((2, 128, 8192), bf16), V((2, 16, 2, 64, 512), bf16), V((2, 2, 2, 64, 128), bf16),
         V((2, 32, 64, 512), bf16), V((2, 32, 64, 256), bf16), V((512, 256), bf16), V((16, 256), bf16),
         V((32, 256), bf16), V((2, 16, 4, 16, 256), bf16), V((2, 16, 4, 16, 256), bf16), V((2, 2, 2, 16, 256), bf16),
         V((2, 16, 3, 16, 256), bf16), V((32, 8, 128), f32), V((4, 8, 16, 256), bf16), V((4, 8, 32, 256), bf16),
         DMA((2,))] + [DMA((2, 32))] * 6 + [DMA((32,)), DMA((32,)), DMA((2,)),
         DMA((2, 16)), DMA((2, 16)), DMA((2, 2)), DMA((2, 16)), DMA((2, 32)), DMA((2, 16)), DMA((2, 2, 4)),
         DMA((2, 2, 4)), DMA((8,)), DMA((8,)), DMA((8,)), DMA((8,)), DMA((4,)), DMA((4,)), DMA((4,)), DMA((4,)),
         DMA((32,)), DMA((32,))],
        1,
    )
    k_new, c_new, km_new, cm_new, k_half, c_half = call(
        advance_body, "advance",
        (token_counts, traces, h, u, grams, k_factor, c_factor, k_moment, c_moment, leads), [SM] + [VM] * 9,
        [((1, 256, 512), f32)] * 4 + [((512, 256), bf16)] * 2, [VM] * 6,
    )
    (precond,) = call(
        precond_body, "precond", (k_half, c_half, grad_weight, grad_lead), [VM] * 4, [((1024, 256), bf16)], [VM],
        [V((32, 32, 256), bf16), V((32, 32, 256), bf16), V((1024, 256), f32), V((32, 256), bf16),
         V((32, 32, 256), bf16), V((1024, 256), bf16), V((256, 256), bf16), V((4, 4, 128, 256), bf16),
         V((256, 256), bf16), V((8, 256, 256), bf16), V((4, 256, 256), f32),
         DMA((32,)), DMA((32,)), DMA, DMA((32,)), DMA((4,)), DMA, DMA((8,)), DMA((4,)), DMA((4,)), DMA((4,)),
         DMA((8,)), DMA, DMA, DMA((8,))],
        2,
    )
    return k_new, c_new, km_new, cm_new, precond


def solution(mesh):
    in_specs = (
        P(("dp", "fsdp"), None),
        P(("dp", "fsdp"), None),
        P(),
        P("fsdp", None, None),
        P("fsdp", None, None),
        P("fsdp", None, None),
        P("fsdp", None, None),
        P("dp", "fsdp"),
    )
    out_specs = (
        P("fsdp", None, None),
        P("fsdp", None, None),
        P("fsdp", None, None),
        P("fsdp", None, None),
        P("dp", "fsdp"),
    )
    return jax.shard_map(per_device, mesh=mesh, in_specs=in_specs, out_specs=out_specs, check_vma=False)
```

```python
import functools

import jax
import jax.numpy as jnp
from jax import lax
from jax.experimental import pallas as pl
from jax.experimental.pallas import tpu as pltpu
from jax.sharding import PartitionSpec as P

MESH = pl.DeviceIdType.MESH
highest = lax.Precision.HIGHEST
f32 = jnp.float32
bf16 = jnp.bfloat16

damping = 0.1
momentum_rate = 0.5
step_rate = 0.2

NX, NY, NZ = 4, 4, 8


def position():
    d = lax.axis_index("dp")
    f = lax.axis_index("fsdp")
    return lax.div(f, NZ), lax.div(d, 2), lax.rem(f, NZ), lax.rem(d, 2)


def device(x, y, z, c):
    return (y * 2 + c, x * NZ + z)


def class_of(x, y, z, c):
    return lax.rem(x, 2) * 8 + lax.rem(y, 2) * 4 + c * 2 + lax.rem(z, 2)


def send(src, dst, send_sem, recv_sem, target):
    return pltpu.make_async_remote_copy(
        src_ref=src, dst_ref=dst, send_sem=send_sem, recv_sem=recv_sem, device_id=target, device_id_type=MESH
    )


def arrived(dst, sem):
    pltpu.make_async_copy(dst, dst, sem).wait()


def greet(barrier, target):
    pl.semaphore_signal(barrier, inc=1, device_id=target, device_id_type=MESH)


ANY = pl.BlockSpec(memory_space=pl.ANY)
VM = pl.BlockSpec(memory_space=pltpu.VMEM)
DMA = pltpu.SemaphoreType.DMA


def call(body, name, ins, in_specs, outs, out_specs, scratch=(), cid=None):
    params = dict(collective_id=cid, has_side_effects=True) if cid is not None else {}
    return pl.pallas_call(
        body,
        out_shape=[jax.ShapeDtypeStruct(s, t) for s, t in outs],
        in_specs=in_specs,
        out_specs=out_specs,
        scratch_shapes=list(scratch),
        compiler_params=pltpu.CompilerParams(**params),
        name=name,
    )(*ins)


def dot(a, b):
    return jnp.dot(a, b, precision=highest, preferred_element_type=f32)


def dot16(a, b):
    return jnp.dot(a, b, preferred_element_type=f32)


def dot(a, b):
    return jnp.dot(a, b, precision=highest, preferred_element_type=f32)


def dot16(a, b):
    return jnp.dot(a, b, preferred_element_type=f32)


def step_body(
    counts, acts, grads, k_factor, c_factor, k_moment, c_moment, grad, k_new, c_new, km_new, cm_new, out,
    h_out, u_out, gram_out, lead_src, lead_in, own, lead_sum, all_lead, second, lead_rows, cb, term, terms, part, k_half,
    c_half, raw, xs, ls, xc, x0, b0, piece_b, piece_g, ps, py_in, qx, px_in, qz, pz_in, sm, st, tr, lead_b, lead_g,
    in_s, s1, r1, s2, r2, s5, r4, s3, s4, r3,
    rs_s, rs_r, de_s, de_r, a0_s, a0_r, ag_s, fw_s, zb_s, zb_r, zg_s, zg_r, xb_s, xb_r, xg_s, xg_r, tr_s, tr_r,
    bo_s, bo_r, ga_s, ga_r, ca_s, ca_r, cz_s, cz_r, cx_s, cx_r, ro_s, ro_r, te_s, te_r,
):
    x, y, z, c = position()
    d, f = lax.axis_index("dp"), lax.axis_index("fsdp")
    barrier = pltpu.get_barrier_semaphore()
    loads = [pltpu.make_async_copy(ref, raw.at[i], in_s.at[i]) for i, ref in enumerate((acts, grads))]
    for one in loads:
        one.start()
    partner = device(x, y, z, 1 - c)

    def cell(sign, a, b, g, e):
        return (
            lax.rem(x + sign * a + NX, NX),
            lax.rem(y + sign * b + NY, NY),
            lax.rem(z + sign * g + NZ, NZ),
            lax.rem(c + e, 2),
        )

    offsets = [(a, b, g, e) for a in (0, 1) for b in (0, 1) for g in (0, 1) for e in (0, 1)]
    mine = class_of(x, y, z, c)
    xi, yi, zi = lax.div(x, 2), lax.div(y, 2), lax.div(z, 2)
    slot = yi * 8 + xi * 4 + zi
    mate_y = device(x, lax.rem(y + 2, NY), z, c)
    mate_x = device(lax.rem(x + 2, NX), y, z, c)

    def mate_z(g):
        return device(x, y, lax.rem(z + 2 * g, NZ), c)

    k = lax.rem(f, 16)
    px, py, pc, pz = lax.div(k, 8), lax.rem(lax.div(k, 4), 2), lax.rem(lax.div(k, 2), 2), lax.rem(k, 2)

    def group_for(parity):
        return lax.rem(2 * yi + parity + lax.rem(zi, 2), NY) * 2 + lax.div(zi, 2)

    def slots_at(there_y):
        shift = lax.rem(there_y + py, 2)
        low = lax.div(lax.rem(there_y - shift + NY, NY), 2) * 8 + 2 * c + shift
        return [low, low + 4]

    def owner(j, qx, qy, qz, qc):
        return device(qx + 2 * lax.rem(lax.div(j, 4), 2), qy + 2 * lax.div(j, 8), qz + 2 * lax.rem(j, 4), qc)

    to_d = group_for(lax.rem(y, 2))
    from_j = slots_at(y)

    def is_me(there):
        return jnp.logical_and(there[0] == d, there[1] == f)

    def lead_target(t):
        return (group_for(lax.rem(lax.div(t, 4), 2)), t)

    for sign in (1, -1):
        for o in offsets:
            if o[:3] == (0, 0, 0) and (o[3] == 0 or sign == -1):
                continue
            greet(barrier, device(*cell(sign, *o)))
    for there in (mate_y, mate_x, mate_z(1), mate_z(2), mate_z(3)):
        greet(barrier, there)

    @pl.loop(1, 32)
    def _(t):
        greet(barrier, (d, lax.rem(f + t, 32)))

    for t in range(1, 4):
        greet(barrier, device(x, lax.rem(y + t, NY), z, c))
    for j in from_j:
        for there in (owner(j, px, py, pz, pc), owner(j, 0, 0, 0, 0)):

            @pl.when(jnp.logical_not(is_me(there)))
            def _():
                greet(barrier, there)

    @pl.when(d == 0)
    def _():
        for t in range(1, 8):
            greet(barrier, (t, f))

    @pl.when(d > 0)
    def _():
        greet(barrier, (0, f))

    limit = counts[0] * jnp.where(d == 0, 1, 0)
    for i in range(1, 8):
        limit = limit + counts[i] * jnp.where(d == i, 1, 0)
    kept = []
    for h in range(2):
        at_slot = lax.broadcasted_iota(jnp.int32, (64, 256), 0) + (f * 128 + h * 64)
        kept.append(jnp.where(at_slot < limit, 1.0, 0.0).astype(bf16))

    def mask(side):
        loads[side].wait()
        for h in range(2):
            rows = slice(h * 64, h * 64 + 64)
            lead = raw[side, rows, 0:256] * kept[h]
            ls[side, 0, h, :, :] = lead[:, 0:128]
            ls[side, 1, h, :, :] = lead[:, 128:256]
            for i in range(16):
                for m in range(2):
                    n = m * 16 + i
                    cols = slice(m * 256, m * 256 + 256)
                    xs[side, i, h, :, cols] = raw[side, rows, n * 256 : n * 256 + 256] * kept[h]

    half = pl.ds(pl.multiple_of(c * 128, 128), 128)
    other_half = pl.ds(pl.multiple_of(128 - c * 128, 128), 128)

    def exchange(side):
        copies = []
        for i in (14, 15, 12, 13, 10, 11, 6, 7, 8, 9, 4, 5, 2, 3, 1, 0):
            for h, sign in ((0, 1), (1, -1)):
                there = cell(sign, *offsets[i])
                to = class_of(*there)
                at = h * 16 + i
                if i == 0:
                    one = pltpu.make_async_copy(xs.at[side, to, h], xc.at[side, at], r1.at[side, at])
                    two = pltpu.make_async_copy(ls.at[side, c, h], x0.at[side, at, :, half], r2.at[side, at])
                else:
                    tc = there[3]
                    to_half = pl.ds(pl.multiple_of(tc * 128, 128), 128)
                    dst = device(*there)
                    one = send(xs.at[side, to, h], xc.at[side, at], s1.at[side, at], r1.at[side, at], dst)
                    two = send(ls.at[side, tc, h], x0.at[side, at, :, to_half], s2.at[side, at], r2.at[side, at], dst)
                two.start()
                one.start()
                copies.append((i, at, one, two))
        return copies

    def collect(side, copies):
        passed = []
        for i, at, one, two in copies:
            got = x0.at[side, at, :, half]
            arrived(got, r2.at[side, at])
            on = send(got, x0.at[side, at ^ 1, :, half], s5.at[side, at], r4.at[side, at ^ 1], partner)
            on.start()
            passed.append(on)
        for i, at, one, two in copies:
            arrived(xc.at[side, at], r1.at[side, at])
        for i, at, one, two in copies:
            arrived(x0.at[side, at, :, other_half], r4.at[side, at])
        return passed

    def grad_piece(t):
        return grad.at[pl.ds(pl.multiple_of(t * 32, 32), 32)]

    def lead_piece(t):
        return b0.at[pl.ds(pl.multiple_of(t * 16, 16), 16)]

    @pl.when(f == 0)
    def _():
        b0[0:256, :] = k_factor[0, :, 0:256].astype(bf16)
        b0[256:512, :] = c_factor[0, :, 0:256].astype(bf16)

    mask(0)
    to_self = jnp.where(is_me((to_d, mine)), 1, 0) + jnp.where(is_me((to_d, mine + 16)), 1, 0)
    lead_self = jnp.where(is_me(lead_target(f)), 1, 0)
    pl.semaphore_wait(
        barrier, 29 + 5 + 31 + 3 + 2 - to_self + jnp.where(mine == 0, 32 - lead_self, 0) + jnp.where(d == 0, 7, 1)
    )
    tokens = [exchange(0)]
    mask(1)
    tokens.append(exchange(1))

    @pl.when(f == 0)
    def _():
        pltpu.make_async_copy(grad_piece(0), piece_g, r3.at[0]).start()
        pltpu.make_async_copy(lead_piece(0), piece_b, r3.at[1]).start()

        @pl.loop(1, 32)
        def _(t):
            send(grad_piece(t), piece_g, s3.at[t], r3.at[0], (d, t)).start()
            send(lead_piece(t), piece_b, s4.at[t], r3.at[1], (d, t)).start()


    flag = jnp.where(f > 0, 1.0, 0.0)
    for side, factor in enumerate((k_factor, c_factor)):
        diag = factor[0, :, 0:256]
        border = factor[0, :, 256:512] * flag
        gram_out[side] = dot(diag.T, diag) + dot(border.T, border)
        tr_g = jnp.sum(diag * diag) + jnp.sum(border * border)
        tr[f, side * 2 + 1 : side * 2 + 2, :] = jnp.full((1, 128), tr_g, f32)
    tr[f, 4:8, :] = jnp.zeros((4, 128), f32)

    dims = (((0,), (0,)), ((), ()))

    def gram(side):
        lead = x0[side].reshape(2048, 256)
        a = xc[side, :, :, 0:256].reshape(2048, 256)
        b = xc[side, :, :, 256:512].reshape(2048, 256)
        for i, (left, right) in enumerate(((a, a), (b, b), (lead, a), (lead, b))):
            g = lax.dot_general(left, right, dims, preferred_element_type=f32)
            ps[side, :, i, :, :] = g.astype(bf16).reshape(16, 16, 256)

    def y_copy(side):
        src = ps.at[side, pl.ds((1 - yi) * 8, 8)]
        return send(src, py_in.at[side], rs_s.at[side, 0], rs_r.at[side, 0], mate_y)

    def x_copy(side):
        src = qx.at[side, pl.ds((1 - xi) * 4, 4)]
        return send(src, px_in.at[side], rs_s.at[side, 1], rs_r.at[side, 1], mate_x)

    def z_copy(side, g):
        src = qz.at[side, lax.rem(zi + g, 4)]
        return send(src, pz_in.at[side, g], rs_s.at[side, 1 + g], rs_r.at[side, 1 + g], mate_z(g))

    def over_x(side):
        arrived(py_in.at[side], rs_r.at[side, 0])
        qx[side] = (ps[side, pl.ds(yi * 8, 8)].astype(f32) + py_in[side].astype(f32)).astype(bf16)
        x_copy(side).start()

    def over_z(side):
        arrived(px_in.at[side], rs_r.at[side, 1])
        qz[side] = (qx[side, pl.ds(xi * 4, 4)].astype(f32) + px_in[side].astype(f32)).astype(bf16)
        for g in range(1, 4):
            z_copy(side, g).start()

    passed = collect(0, tokens[0])
    gram(0)
    y_copy(0).start()
    passed += collect(1, tokens[1])
    gram(1)
    y_copy(1).start()
    def total(side):
        value = qz[side, zi].astype(f32)
        for g in range(1, 4):
            arrived(pz_in.at[side, g], rs_r.at[side, 1 + g])
            value = value + pz_in[side, g].astype(f32)
        value = value.astype(bf16)
        for m in range(2):
            for q in range(2):
                sm[side, m, q] = value[2 * q + m]

    def lead_send(side, t):
        return send(sm.at[side, 0, 0], st.at[side, slot, 2], a0_s.at[side, t], a0_r.at[side, slot], lead_target(t))

    def rows_send(side, m):
        there = (to_d, mine + 16 * m)
        return send(sm.at[side, m], st.at[side, slot, 0:2], de_s.at[side, m], de_r.at[side, slot], there)

    def deliver(side):
        @pl.when(mine == 0)
        def _():
            @pl.loop(0, 32)
            def _(t):
                me = is_me(lead_target(t))

                @pl.when(me)
                def _():
                    pltpu.make_async_copy(sm.at[side, 0, 0], st.at[side, slot, 2], a0_r.at[side, slot]).start()

                @pl.when(jnp.logical_not(me))
                def _():
                    lead_send(side, t).start()

        for m in range(2):
            me = is_me((to_d, mine + 16 * m))

            @pl.when(me)
            def _():
                pltpu.make_async_copy(sm.at[side, m], st.at[side, slot, 0:2], de_r.at[side, slot]).start()

            @pl.when(jnp.logical_not(me))
            def _():
                rows_send(side, m).start()

    def share_send(side, i, t):
        there = device(x, lax.rem(y + t, NY), z, c) if t > 0 else partner
        at = st.at[side, from_j[i]]
        return send(at, at, ag_s.at[side, i, t], de_r.at[side, from_j[i]], there)

    def pass_send(side, i, t):
        j = slots_at(lax.rem(y + NY - t, NY))[i]
        return send(st.at[side, j], st.at[side, j], fw_s.at[side, i, t], de_r.at[side, j], partner)

    def share(side):
        for i in range(2):
            arrived(st.at[side, from_j[i], 0:2], de_r.at[side, from_j[i]])
            arrived(st.at[side, from_j[i], 2], a0_r.at[side, from_j[i]])
            for t in (1, 2, 3, 0):
                share_send(side, i, t).start()

    def pass_on(side):
        for t in (1, 3, 2):
            for i in range(2):
                j = slots_at(lax.rem(y + NY - t, NY))[i]
                arrived(st.at[side, j], de_r.at[side, j])
                pass_send(side, i, t).start()

    over_x(0)
    arrived(piece_g, r3.at[0])
    arrived(piece_b, r3.at[1])
    own_b = pltpu.make_async_copy(piece_b, lead_b.at[x, z], zb_r.at[0])
    own_g = pltpu.make_async_copy(piece_g, lead_g.at[x, z], zg_r.at[0])
    own_b.start()
    own_g.start()
    for t in range(1, 8):
        there = (d, x * NZ + lax.rem(z + t, NZ))
        send(piece_b, lead_b.at[x, z], zb_s.at[t], zb_r.at[t], there).start()
        send(piece_g, lead_g.at[x, z], zg_s.at[t], zg_r.at[t], there).start()
    over_x(1)
    over_z(0)
    over_z(1)
    total(0)
    deliver(0)
    total(1)
    deliver(1)
    own_b.wait()
    own_g.wait()
    for t in range(1, 8):
        there = (d, x * NZ + lax.rem(z + t, NZ))
        behind = lax.rem(z + NZ - t, NZ)
        send(piece_b, lead_b.at[x, z], zb_s.at[t], zb_r.at[t], there).wait_send()
        send(piece_g, lead_g.at[x, z], zg_s.at[t], zg_r.at[t], there).wait_send()
        arrived(lead_b.at[x, behind], zb_r.at[t])
        arrived(lead_g.at[x, behind], zg_r.at[t])
    for t in range(1, 4):
        there = (d, lax.rem(x + t, NX) * NZ + z)
        send(lead_b.at[x], lead_b.at[x], xb_s.at[t], xb_r.at[t], there).start()
        send(lead_g.at[x], lead_g.at[x], xg_s.at[t], xg_r.at[t], there).start()
    share(0)
    share(1)
    pass_on(0)
    pass_on(1)

    rows = lax.broadcasted_iota(jnp.int32, (256, 256), 0)
    cols = lax.broadcasted_iota(jnp.int32, (256, 256), 1)

    def second_moment(side):
        for j in range(16):
            @pl.when(lax.div(j % 4, 2) != c)
            def _():
                arrived(st.at[side, j], de_r.at[side, j])

        factor = (k_factor, c_factor)[side]
        diag16 = factor[0, :, 0:256].astype(bf16)
        border16 = (factor[0, :, 256:512] * flag).astype(bf16)
        a = st[side, :, 0].reshape(256, 256)
        cross = st[side, :, 1].reshape(256, 256)
        lead = st[side, :, 2].reshape(256, 256)
        u = dot16(cross, diag16) + dot16(lead, border16)
        v = dot16(a, diag16) + dot16(cross.T, border16)
        h = dot(diag16.astype(f32).T, v) + dot(border16.astype(f32).T, u)
        u_out[side] = u
        h_out[side] = h
        tr[f, side * 2 : side * 2 + 1, :] = jnp.full((1, 128), jnp.sum(jnp.where(rows == cols, h, 0.0)), f32)

    second_moment(0)
    second_moment(1)

    @pl.loop(1, 32)
    def _(t):
        send(tr.at[f], tr.at[f], tr_s.at[t], tr_r.at[t], (d, lax.rem(f + t, 32))).start()

    for t in range(1, 4):
        there = (d, lax.rem(x + t, NX) * NZ + z)
        behind = lax.rem(x + NX - t, NX)
        send(lead_b.at[x], lead_b.at[x], xb_s.at[t], xb_r.at[t], there).wait_send()
        send(lead_g.at[x], lead_g.at[x], xg_s.at[t], xg_r.at[t], there).wait_send()
        arrived(lead_b.at[behind], xb_r.at[t])
        arrived(lead_g.at[behind], xg_r.at[t])

    @pl.loop(1, 32)
    def _(t):
        send(tr.at[f], tr.at[f], tr_s.at[t], tr_r.at[t], (d, lax.rem(f + t, 32))).wait_send()
        arrived(tr.at[lax.rem(f + 32 - t, 32)], tr_r.at[t])

    sums_all = tr[0]
    for i in range(1, 32):
        sums_all = sums_all + tr[i]
    trace = [sums_all[i : i + 1, 0:1] for i in range(4)]
    total_tokens = counts[0]
    for i in range(1, 8):
        total_tokens = total_tokens + counts[i]
    inverse = 1.0 / jnp.full((1, 1), total_tokens.astype(f32), f32)
    width = 8192.0
    identity = jnp.where(rows == cols, 1.0, 0.0)

    def advance(side):
        factor, moment = (k_factor, c_factor)[side], (k_moment, c_moment)[side]
        f_new, m_new, half16 = (k_new, c_new)[side], (km_new, cm_new)[side], (k_half, c_half)[side]
        other_h = trace[2 - 2 * side] * inverse * inverse
        other_g = trace[3 - 2 * side] * damping
        diag = factor[0, :, 0:256]
        border = factor[0, :, 256:512] * flag
        lead = lead_b[...].reshape(512, 256)[side * 256 : side * 256 + 256, :].astype(f32)
        fresh = (other_h * h_out[side] + other_g * gram_out[side] - width * identity) / (2.0 * width)
        cross = dot(lead.T, other_h * u_out[side] + other_g * border) * flag / (2.0 * width)
        m_diag = momentum_rate * moment[0, :, 0:256] + fresh
        m_side = (momentum_rate * moment[0, :, 256:512] + cross) * flag
        n_diag = diag - step_rate * dot(diag, m_diag)
        n_side = (border - step_rate * (dot(lead, m_side) + dot(border, m_diag))) * flag
        f_new[0, :, 0:256] = n_diag
        f_new[0, :, 256:512] = n_side
        m_new[0, :, 0:256] = m_diag
        m_new[0, :, 256:512] = m_side
        half16[0:256, :] = n_diag.astype(bf16)
        half16[256:512, :] = n_side.astype(bf16)

    holder = lax.div(z, 4) == c
    root = jnp.logical_and(holder, x == y)
    j = lax.rem(z, 4)

    def quarter(t):
        return c_half.at[pl.ds(pl.multiple_of(t * 128, 128), 128)]

    def scatter_copy(t):
        to = lax.rem(x + t, NX)
        return send(quarter(to), cb.at[to, j], ca_s.at[t], ca_r, (d, to * NZ + z))

    advance(1)

    @pl.when(root)
    def _():
        for t in range(1, 4):
            scatter_copy(t).start()
        pltpu.make_async_copy(quarter(x), cb.at[x, j], ca_r).start()

    advance(0)
    k_diag, k_side = k_half[0:256, :], k_half[256:512, :]
    first = (dot16(grad[...], k_diag) + dot16(lead_g[...].reshape(1024, 256), k_side)).astype(bf16)
    lead_src[...] = dot16(first, k_side.T).astype(bf16).reshape(32, 32, 256)

    own_piece = pltpu.make_async_copy(lead_src.at[f], lead_in.at[f], bo_r.at[0])
    own_piece.start()

    @pl.loop(1, 32)
    def _(t):
        there = lax.rem(f + t, 32)
        send(lead_src.at[there], lead_in.at[f], bo_s.at[t], bo_r.at[t], (d, there)).start()

    own[...] = dot16(first, k_diag.T)

    def ring_copy(t):
        return send(cb.at[x, j], cb.at[x, j], cz_s.at[t], cz_r.at[j], (d, x * NZ + lax.rem(z + t, NZ)))

    @pl.when(holder)
    def _():
        arrived(cb.at[x, j], ca_r)
        for t in range(1, 8):
            ring_copy(t).start()

    own_piece.wait()

    @pl.loop(1, 32)
    def _(t):
        there = lax.rem(f + t, 32)
        send(lead_src.at[there], lead_in.at[f], bo_s.at[t], bo_r.at[t], (d, there)).wait_send()
        arrived(lead_in.at[lax.rem(f + 32 - t, 32)], bo_r.at[t])

    total = lead_in[0].astype(f32)
    for i in range(1, 32):
        total = total + lead_in[i].astype(f32)
    lead_sum[...] = total.astype(bf16)
    second[...] = own[...].astype(bf16)

    @pl.when(f > 0)
    def _():
        send(lead_sum, all_lead.at[f], ga_s, ga_r.at[f], (d, 0)).start()

    for i in range(4):

        @pl.when(jnp.logical_or(jnp.logical_not(holder), j != i))
        def _():
            arrived(cb.at[x, i], cz_r.at[i])

    def spread_copy(t):
        return send(cb.at[x], cb.at[x], cx_s.at[t], cx_r.at[t], (d, lax.rem(x + t, NX) * NZ + z))

    for t in range(1, 4):
        spread_copy(t).start()

    @pl.when(f == 0)
    def _():
        all_lead[0] = lead_sum[...]
        for i in range(1, 32):
            arrived(all_lead.at[i], ga_r.at[i])
        second[...] = (own[...] + all_lead[...].reshape(1024, 256).astype(f32)).astype(bf16)

    src = second.at[0:256]

    @pl.when(d == 0)
    def _():
        for t in range(1, 8):
            send(src, lead_rows, ro_s.at[t], ro_r, (t, f)).start()
        pltpu.make_async_copy(src, lead_rows, ro_r).start()

    for t in range(1, 4):
        arrived(cb.at[lax.rem(x + NX - t, NX)], cx_r.at[t])
    for i in range(4):
        diag = cb[0:2, i].reshape(256, 256)
        part[i] = dot16(diag.T, second[i * 256 : i * 256 + 256, :])
    arrived(lead_rows, ro_r)
    sum_term = jnp.zeros((256, 256), f32)
    for i in range(4):
        diag = cb[0:2, i].reshape(256, 256)
        side = cb[2:4, i].reshape(256, 256)
        third = (part[i] + dot16(side.T, lead_rows[...])).astype(bf16)
        own[i * 256 : i * 256 + 256, :] = dot16(diag, third)
        sum_term = sum_term + dot16(side, third)
    term[...] = sum_term.astype(bf16)

    @pl.when(d > 0)
    def _():
        send(term, terms.at[d], te_s, te_r.at[d], (0, f)).start()

    out[256:1024, :] = own[256:1024, :].astype(bf16)

    @pl.when(d > 0)
    def _():
        out[0:256, :] = own[0:256, :].astype(bf16)
        send(term, terms.at[d], te_s, te_r.at[d], (0, f)).wait_send()

    @pl.when(d == 0)
    def _():
        whole = own[0:256, :] + sum_term
        for t in range(1, 8):
            arrived(terms.at[t], te_r.at[t])
            whole = whole + terms[t].astype(f32)
        out[0:256, :] = whole.astype(bf16)
        for t in range(1, 8):
            send(src, lead_rows, ro_s.at[t], ro_r, (t, f)).wait_send()

    @pl.when(root)
    def _():
        for t in range(1, 4):
            scatter_copy(t).wait_send()

    @pl.when(holder)
    def _():
        for t in range(1, 8):
            ring_copy(t).wait_send()

    for t in range(1, 4):
        spread_copy(t).wait_send()

    @pl.when(f > 0)
    def _():
        send(lead_sum, all_lead.at[f], ga_s, ga_r.at[f], (d, 0)).wait_send()
    for on in passed:
        on.wait_send()
    for side in range(2):
        y_copy(side).wait_send()
        x_copy(side).wait_send()
        for g in range(1, 4):
            z_copy(side, g).wait_send()
    for copies in tokens:
        for i, at, one, two in copies:
            if i > 0:
                one.wait_send()
                two.wait_send()

    @pl.when(f == 0)
    def _():
        @pl.loop(1, 32)
        def _(t):
            send(grad_piece(t), piece_g, s3.at[t], r3.at[0], (d, t)).wait_send()
            send(lead_piece(t), piece_b, s4.at[t], r3.at[1], (d, t)).wait_send()

    for side in range(2):

        @pl.when(mine == 0)
        def _():
            @pl.loop(0, 32)
            def _(t):
                @pl.when(jnp.logical_not(is_me(lead_target(t))))
                def _():
                    lead_send(side, t).wait_send()

        for m in range(2):

            @pl.when(jnp.logical_not(is_me((to_d, mine + 16 * m))))
            def _():
                rows_send(side, m).wait_send()

        for i in range(2):
            for t in range(4):
                share_send(side, i, t).wait_send()
            for t in range(1, 4):
                pass_send(side, i, t).wait_send()


def finish_body(*refs):
    for src, dst in zip(refs[:5], refs[5:]):
        dst[...] = src[...]


def per_device(acts, out_grads, token_counts, k_factor, c_factor, k_moment, c_moment, grad_weight):
    SM = pl.BlockSpec(memory_space=pltpu.SMEM)
    V = pltpu.VMEM
    results = [((1, 256, 512), f32)] * 4 + [((1024, 256), bf16)]
    held = call(
        step_body, "step",
        (token_counts, acts, out_grads, k_factor, c_factor, k_moment, c_moment, grad_weight),
        [SM, ANY, ANY] + [VM] * 5, results, [VM] * 5,
        [V((2, 256, 256), f32), V((2, 256, 256), f32), V((2, 256, 256), f32),
         V((32, 32, 256), bf16), V((32, 32, 256), bf16), V((1024, 256), f32), V((32, 256), bf16),
         V((32, 32, 256), bf16), V((1024, 256), bf16), V((256, 256), bf16), V((4, 4, 128, 256), bf16),
         V((256, 256), bf16), V((8, 256, 256), bf16), V((4, 256, 256), f32), V((512, 256), bf16), V((512, 256), bf16),
         V((2, 128, 8192), bf16), V((2, 16, 2, 64, 512), bf16), V((2, 2, 2, 64, 128), bf16),
         V((2, 32, 64, 512), bf16), V((2, 32, 64, 256), bf16), V((512, 256), bf16), V((16, 256), bf16),
         V((32, 256), bf16), V((2, 16, 4, 16, 256), bf16), V((2, 8, 4, 16, 256), bf16), V((2, 8, 4, 16, 256), bf16),
         V((2, 4, 4, 16, 256), bf16), V((2, 4, 4, 16, 256), bf16), V((2, 4, 4, 16, 256), bf16), V((2, 2, 2, 16, 256), bf16),
         V((2, 16, 3, 16, 256), bf16), V((32, 8, 128), f32), V((4, 8, 16, 256), bf16), V((4, 8, 32, 256), bf16),
         DMA((2,))] + [DMA((2, 32))] * 6 + [DMA((32,)), DMA((32,)), DMA((2,)),
         DMA((2, 16)), DMA((2, 16)), DMA((2, 2)), DMA((2, 16)), DMA((2, 32)), DMA((2, 16)), DMA((2, 2, 4)),
         DMA((2, 2, 4)), DMA((8,)), DMA((8,)), DMA((8,)), DMA((8,)), DMA((4,)), DMA((4,)), DMA((4,)), DMA((4,)),
         DMA((32,)), DMA((32,)),
         DMA((32,)), DMA((32,)), DMA, DMA((32,)), DMA((4,)), DMA, DMA((8,)), DMA((4,)), DMA((4,)), DMA((4,)),
         DMA((8,)), DMA, DMA, DMA((8,))],
        0,
    )
    return tuple(call(finish_body, "finish", held, [VM] * 5, results, [VM] * 5))


def solution(mesh):
    in_specs = (
        P(("dp", "fsdp"), None),
        P(("dp", "fsdp"), None),
        P(),
        P("fsdp", None, None),
        P("fsdp", None, None),
        P("fsdp", None, None),
        P("fsdp", None, None),
        P("dp", "fsdp"),
    )
    out_specs = (
        P("fsdp", None, None),
        P("fsdp", None, None),
        P("fsdp", None, None),
        P("fsdp", None, None),
        P("dp", "fsdp"),
    )
    return jax.shard_map(per_device, mesh=mesh, in_specs=in_specs, out_specs=out_specs, check_vma=False)
```

```python
import functools

import jax
import jax.numpy as jnp
from jax import lax
from jax.experimental import pallas as pl
from jax.experimental.pallas import tpu as pltpu
from jax.sharding import PartitionSpec as P

MESH = pl.DeviceIdType.MESH
highest = lax.Precision.HIGHEST
f32 = jnp.float32
bf16 = jnp.bfloat16

damping = 0.1
momentum_rate = 0.5
step_rate = 0.2

NX, NY, NZ = 4, 4, 8


def position():
    d = lax.axis_index("dp")
    f = lax.axis_index("fsdp")
    return lax.div(f, NZ), lax.div(d, 2), lax.rem(f, NZ), lax.rem(d, 2)


def device(x, y, z, c):
    return (y * 2 + c, x * NZ + z)


def class_of(x, y, z, c):
    return lax.rem(x, 2) * 8 + lax.rem(y, 2) * 4 + c * 2 + lax.rem(z, 2)


def send(src, dst, send_sem, recv_sem, target):
    return pltpu.make_async_remote_copy(
        src_ref=src, dst_ref=dst, send_sem=send_sem, recv_sem=recv_sem, device_id=target, device_id_type=MESH
    )


def arrived(dst, sem):
    pltpu.make_async_copy(dst, dst, sem).wait()


def greet(barrier, target):
    pl.semaphore_signal(barrier, inc=1, device_id=target, device_id_type=MESH)


ANY = pl.BlockSpec(memory_space=pl.ANY)
VM = pl.BlockSpec(memory_space=pltpu.VMEM)
DMA = pltpu.SemaphoreType.DMA


def call(body, name, ins, in_specs, outs, out_specs, scratch=(), cid=None):
    params = dict(collective_id=cid, has_side_effects=True) if cid is not None else {}
    return pl.pallas_call(
        body,
        out_shape=[jax.ShapeDtypeStruct(s, t) for s, t in outs],
        in_specs=in_specs,
        out_specs=out_specs,
        scratch_shapes=list(scratch),
        compiler_params=pltpu.CompilerParams(**params),
        name=name,
    )(*ins)


def dot(a, b):
    return jnp.dot(a, b, precision=highest, preferred_element_type=f32)


def dot16(a, b):
    return jnp.dot(a, b, preferred_element_type=f32)


def dot(a, b):
    return jnp.dot(a, b, precision=highest, preferred_element_type=f32)


def dot16(a, b):
    return jnp.dot(a, b, preferred_element_type=f32)


def step_body(
    counts, acts, grads, k_factor, c_factor, k_moment, c_moment, grad, k_new, c_new, km_new, cm_new, out,
    h_out, u_out, v_out, gram_out, lead_src, lead_in, lead_x, lead_z, own, lead_sum, all_lead, second, lead_rows, cb, term, terms, part, k_half,
    c_half, raw, xs, ls, xc, x0, b0, piece_b, piece_g, ps, py_in, qx, px_in, qz, pz_in, sm, st, tr, lead_b, lead_g,
    in_s, s1, r1, s2, r2, s5, r4, s3, s4, r3,
    rs_s, rs_r, de_s, de_r, a0_s, a0_r, ag_s, fw_s, zb_s, zb_r, zg_s, zg_r, xb_s, xb_r, xg_s, xg_r, tr_s, tr_r,
    bo_s, bo_r, bz_s, bz_r, ga_s, ga_r, ca_s, ca_r, cz_s, cz_r, cx_s, cx_r, ro_s, ro_r, te_s, te_r,
):
    x, y, z, c = position()
    d, f = lax.axis_index("dp"), lax.axis_index("fsdp")
    barrier = pltpu.get_barrier_semaphore()
    loads = [pltpu.make_async_copy(ref, raw.at[i], in_s.at[i]) for i, ref in enumerate((acts, grads))]
    for one in loads:
        one.start()
    partner = device(x, y, z, 1 - c)

    def cell(sign, a, b, g, e):
        return (
            lax.rem(x + sign * a + NX, NX),
            lax.rem(y + sign * b + NY, NY),
            lax.rem(z + sign * g + NZ, NZ),
            lax.rem(c + e, 2),
        )

    offsets = [(a, b, g, e) for a in (0, 1) for b in (0, 1) for g in (0, 1) for e in (0, 1)]
    mine = class_of(x, y, z, c)
    xi, yi, zi = lax.div(x, 2), lax.div(y, 2), lax.div(z, 2)
    slot = (yi * 8 + xi * 4 + zi, xi * 8 + yi * 4 + zi)
    mate_y = device(x, lax.rem(y + 2, NY), z, c)
    mate_x = device(lax.rem(x + 2, NX), y, z, c)

    def mate_z(g):
        return device(x, y, lax.rem(z + 2 * g, NZ), c)

    k = lax.rem(f, 16)
    px, py, pc, pz = lax.div(k, 8), lax.rem(lax.div(k, 4), 2), lax.rem(lax.div(k, 2), 2), lax.rem(k, 2)

    def group_for(parity):
        return lax.rem(2 * yi + parity + lax.rem(zi, 2), NY) * 2 + lax.div(zi, 2)

    def slots_at(there_y, side):
        shift = lax.rem(there_y + py, 2)
        half_y = lax.div(lax.rem(there_y - shift + NY, NY), 2)
        low = half_y * (8, 4)[side] + 2 * c + shift
        return [low, low + (4, 8)[side]]

    def owner(j, qx, qy, qz, qc):
        return device(qx + 2 * lax.rem(lax.div(j, 4), 2), qy + 2 * lax.div(j, 8), qz + 2 * lax.rem(j, 4), qc)

    to_d = group_for(lax.rem(y, 2))
    from_j = [slots_at(y, side) for side in range(2)]

    def is_me(there):
        return jnp.logical_and(there[0] == d, there[1] == f)

    def lead_target(t):
        return (group_for(lax.rem(lax.div(t, 4), 2)), t)

    for sign in (1, -1):
        for o in offsets:
            if o[:3] == (0, 0, 0) and (o[3] == 0 or sign == -1):
                continue
            greet(barrier, device(*cell(sign, *o)))
    for there in (mate_y, mate_x, mate_z(1), mate_z(2), mate_z(3)):
        greet(barrier, there)

    @pl.loop(1, 32)
    def _(t):
        greet(barrier, (d, lax.rem(f + t, 32)))

    for t in range(1, 4):
        greet(barrier, device(x, lax.rem(y + t, NY), z, c))
    for j in from_j[0]:
        for there in (owner(j, px, py, pz, pc), owner(j, 0, 0, 0, 0)):

            @pl.when(jnp.logical_not(is_me(there)))
            def _():
                greet(barrier, there)

    @pl.when(d == 0)
    def _():
        for t in range(1, 8):
            greet(barrier, (t, f))

    @pl.when(d > 0)
    def _():
        greet(barrier, (0, f))

    limit = counts[0] * jnp.where(d == 0, 1, 0)
    for i in range(1, 8):
        limit = limit + counts[i] * jnp.where(d == i, 1, 0)
    kept = []
    for h in range(2):
        at_slot = lax.broadcasted_iota(jnp.int32, (64, 256), 0) + (f * 128 + h * 64)
        kept.append(jnp.where(at_slot < limit, 1.0, 0.0).astype(bf16))

    def mask(side):
        loads[side].wait()
        for h in range(2):
            rows = slice(h * 64, h * 64 + 64)
            lead = raw[side, rows, 0:256] * kept[h]
            ls[side, 0, h, :, :] = lead[:, 0:128]
            ls[side, 1, h, :, :] = lead[:, 128:256]
            for i in range(16):
                for m in range(2):
                    n = m * 16 + i
                    cols = slice(m * 256, m * 256 + 256)
                    xs[side, i, h, :, cols] = raw[side, rows, n * 256 : n * 256 + 256] * kept[h]

    half = pl.ds(pl.multiple_of(c * 128, 128), 128)
    other_half = pl.ds(pl.multiple_of(128 - c * 128, 128), 128)

    def exchange(side):
        copies = []
        for i in (14, 15, 12, 13, 10, 11, 6, 7, 8, 9, 4, 5, 2, 3, 1, 0):
            for h, sign in ((0, 1), (1, -1)):
                there = cell(sign, *offsets[i])
                to = class_of(*there)
                at = h * 16 + i
                if i == 0:
                    one = pltpu.make_async_copy(xs.at[side, to, h], xc.at[side, at], r1.at[side, at])
                    two = pltpu.make_async_copy(ls.at[side, c, h], x0.at[side, at, :, half], r2.at[side, at])
                else:
                    tc = there[3]
                    to_half = pl.ds(pl.multiple_of(tc * 128, 128), 128)
                    dst = device(*there)
                    one = send(xs.at[side, to, h], xc.at[side, at], s1.at[side, at], r1.at[side, at], dst)
                    two = send(ls.at[side, tc, h], x0.at[side, at, :, to_half], s2.at[side, at], r2.at[side, at], dst)
                two.start()
                one.start()
                copies.append((i, at, one, two))
        return copies

    def collect(side, copies):
        passed = []
        for i, at, one, two in copies:
            got = x0.at[side, at, :, half]
            arrived(got, r2.at[side, at])
            on = send(got, x0.at[side, at ^ 1, :, half], s5.at[side, at], r4.at[side, at ^ 1], partner)
            on.start()
            passed.append(on)
        for i, at, one, two in copies:
            arrived(xc.at[side, at], r1.at[side, at])
        for i, at, one, two in copies:
            arrived(x0.at[side, at, :, other_half], r4.at[side, at])
        return passed

    def grad_piece(t):
        return grad.at[pl.ds(pl.multiple_of(t * 32, 32), 32)]

    def lead_piece(t):
        return b0.at[pl.ds(pl.multiple_of(t * 16, 16), 16)]

    @pl.when(f == 0)
    def _():
        b0[0:256, :] = k_factor[0, :, 0:256].astype(bf16)
        b0[256:512, :] = c_factor[0, :, 0:256].astype(bf16)

    mask(0)
    to_self = jnp.where(is_me((to_d, mine)), 1, 0) + jnp.where(is_me((to_d, mine + 16)), 1, 0)
    lead_self = jnp.where(is_me(lead_target(f)), 1, 0)
    pl.semaphore_wait(
        barrier, 29 + 5 + 31 + 3 + 2 - to_self + jnp.where(mine == 0, 32 - lead_self, 0) + jnp.where(d == 0, 7, 1)
    )
    tokens = [exchange(0)]
    mask(1)
    tokens.append(exchange(1))

    @pl.when(f == 0)
    def _():
        pltpu.make_async_copy(grad_piece(0), piece_g, r3.at[0]).start()
        pltpu.make_async_copy(lead_piece(0), piece_b, r3.at[1]).start()

        @pl.loop(1, 32)
        def _(t):
            send(grad_piece(t), piece_g, s3.at[t], r3.at[0], (d, t)).start()
            send(lead_piece(t), piece_b, s4.at[t], r3.at[1], (d, t)).start()


    flag = jnp.where(f > 0, 1.0, 0.0)
    for side, factor in enumerate((k_factor, c_factor)):
        diag = factor[0, :, 0:256]
        border = factor[0, :, 256:512] * flag
        gram_out[side] = dot(diag.T, diag) + dot(border.T, border)
        tr_g = jnp.sum(diag * diag) + jnp.sum(border * border)
        tr[f, side * 2 + 1 : side * 2 + 2, :] = jnp.full((1, 128), tr_g, f32)
    tr[f, 4:8, :] = jnp.zeros((4, 128), f32)

    dims = (((0,), (0,)), ((), ()))

    def gram(side):
        lead = x0[side].reshape(2048, 256)
        a = xc[side, :, :, 0:256].reshape(2048, 256)
        b = xc[side, :, :, 256:512].reshape(2048, 256)
        for i, (left, right) in enumerate(((a, a), (b, b), (lead, a), (lead, b))):
            g = lax.dot_general(left, right, dims, preferred_element_type=f32)
            ps[side, :, i, :, :] = g.astype(bf16).reshape(16, 16, 256)

    bits = ((yi, xi), (xi, yi))
    halves = ((mate_y, mate_x), (mate_x, mate_y))

    def half_copy(side):
        src = ps.at[side, pl.ds((1 - bits[side][0]) * 8, 8)]
        return send(src, py_in.at[side], rs_s.at[side, 0], rs_r.at[side, 0], halves[side][0])

    def quarter_copy(side):
        src = qx.at[side, pl.ds((1 - bits[side][1]) * 4, 4)]
        return send(src, px_in.at[side], rs_s.at[side, 1], rs_r.at[side, 1], halves[side][1])

    def z_copy(side, g):
        src = qz.at[side, lax.rem(zi + g, 4)]
        return send(src, pz_in.at[side, g], rs_s.at[side, 1 + g], rs_r.at[side, 1 + g], mate_z(g))

    def over_half(side):
        arrived(py_in.at[side], rs_r.at[side, 0])
        qx[side] = (ps[side, pl.ds(bits[side][0] * 8, 8)].astype(f32) + py_in[side].astype(f32)).astype(bf16)
        quarter_copy(side).start()

    def over_quarter(side):
        arrived(px_in.at[side], rs_r.at[side, 1])
        qz[side] = (qx[side, pl.ds(bits[side][1] * 4, 4)].astype(f32) + px_in[side].astype(f32)).astype(bf16)
        for g in range(1, 4):
            z_copy(side, g).start()

    passed = collect(0, tokens[0])
    gram(0)
    half_copy(0).start()
    passed += collect(1, tokens[1])
    gram(1)
    half_copy(1).start()
    def total(side):
        value = qz[side, zi].astype(f32)
        for g in range(1, 4):
            arrived(pz_in.at[side, g], rs_r.at[side, 1 + g])
            value = value + pz_in[side, g].astype(f32)
        value = value.astype(bf16)
        for m in range(2):
            for q in range(2):
                sm[side, m, q] = value[2 * q + m]

    def lead_send(side, t):
        return send(sm.at[side, 0, 0], st.at[side, slot[side], 2], a0_s.at[side, t], a0_r.at[side, slot[side]], lead_target(t))

    def rows_send(side, m):
        there = (to_d, mine + 16 * m)
        return send(sm.at[side, m], st.at[side, slot[side], 0:2], de_s.at[side, m], de_r.at[side, slot[side]], there)

    def deliver(side):
        @pl.when(mine == 0)
        def _():
            @pl.loop(0, 32)
            def _(t):
                me = is_me(lead_target(t))

                @pl.when(me)
                def _():
                    pltpu.make_async_copy(sm.at[side, 0, 0], st.at[side, slot[side], 2], a0_r.at[side, slot[side]]).start()

                @pl.when(jnp.logical_not(me))
                def _():
                    lead_send(side, t).start()

        for m in range(2):
            me = is_me((to_d, mine + 16 * m))

            @pl.when(me)
            def _():
                pltpu.make_async_copy(sm.at[side, m], st.at[side, slot[side], 0:2], de_r.at[side, slot[side]]).start()

            @pl.when(jnp.logical_not(me))
            def _():
                rows_send(side, m).start()

    def share_send(side, i, t):
        there = device(x, lax.rem(y + t, NY), z, c) if t > 0 else partner
        at = st.at[side, from_j[side][i]]
        return send(at, at, ag_s.at[side, i, t], de_r.at[side, from_j[side][i]], there)

    def pass_send(side, i, t):
        j = slots_at(lax.rem(y + NY - t, NY), side)[i]
        return send(st.at[side, j], st.at[side, j], fw_s.at[side, i, t], de_r.at[side, j], partner)

    def share(side):
        for i in range(2):
            arrived(st.at[side, from_j[side][i], 0:2], de_r.at[side, from_j[side][i]])
            arrived(st.at[side, from_j[side][i], 2], a0_r.at[side, from_j[side][i]])
            for t in (1, 2, 3, 0):
                share_send(side, i, t).start()

    def pass_on(side):
        for t in (1, 3, 2):
            for i in range(2):
                j = slots_at(lax.rem(y + NY - t, NY), side)[i]
                arrived(st.at[side, j], de_r.at[side, j])
                pass_send(side, i, t).start()

    over_half(0)
    arrived(piece_g, r3.at[0])
    arrived(piece_b, r3.at[1])
    own_b = pltpu.make_async_copy(piece_b, lead_b.at[x, z], zb_r.at[0])
    own_g = pltpu.make_async_copy(piece_g, lead_g.at[x, z], zg_r.at[0])
    own_b.start()
    own_g.start()
    for t in range(1, 8):
        there = (d, x * NZ + lax.rem(z + t, NZ))
        send(piece_b, lead_b.at[x, z], zb_s.at[t], zb_r.at[t], there).start()
        send(piece_g, lead_g.at[x, z], zg_s.at[t], zg_r.at[t], there).start()
    over_half(1)
    over_quarter(0)
    over_quarter(1)
    total(0)
    deliver(0)
    total(1)
    deliver(1)
    own_b.wait()
    own_g.wait()
    for t in range(1, 8):
        there = (d, x * NZ + lax.rem(z + t, NZ))
        behind = lax.rem(z + NZ - t, NZ)
        send(piece_b, lead_b.at[x, z], zb_s.at[t], zb_r.at[t], there).wait_send()
        send(piece_g, lead_g.at[x, z], zg_s.at[t], zg_r.at[t], there).wait_send()
        arrived(lead_b.at[x, behind], zb_r.at[t])
        arrived(lead_g.at[x, behind], zg_r.at[t])
    for t in range(1, 4):
        there = (d, lax.rem(x + t, NX) * NZ + z)
        send(lead_b.at[x], lead_b.at[x], xb_s.at[t], xb_r.at[t], there).start()
        send(lead_g.at[x], lead_g.at[x], xg_s.at[t], xg_r.at[t], there).start()
    share(0)
    share(1)
    pass_on(0)
    pass_on(1)

    rows = lax.broadcasted_iota(jnp.int32, (256, 256), 0)
    cols = lax.broadcasted_iota(jnp.int32, (256, 256), 1)

    def second_moment(side):
        for j in range(16):
            @pl.when(lax.div(j % 4, 2) != c)
            def _():
                arrived(st.at[side, j], de_r.at[side, j])

        factor = (k_factor, c_factor)[side]
        diag16 = factor[0, :, 0:256].astype(bf16)
        border16 = (factor[0, :, 256:512] * flag).astype(bf16)
        a = st[side, :, 0].reshape(256, 256)
        cross = st[side, :, 1].reshape(256, 256)
        lead = st[side, :, 2].reshape(256, 256)
        u = dot16(cross, diag16) + dot16(lead, border16)
        v = dot16(a, diag16) + dot16(cross.T, border16)
        tr_h = jnp.sum(diag16.astype(f32) * v) + jnp.sum(border16.astype(f32) * u)
        tr[f, side * 2 : side * 2 + 1, :] = jnp.full((1, 128), tr_h, f32)
        u_out[side] = u
        v_out[side] = v

    second_moment(0)
    second_moment(1)

    @pl.loop(1, 32)
    def _(t):
        send(tr.at[f], tr.at[f], tr_s.at[t], tr_r.at[t], (d, lax.rem(f + t, 32))).start()

    for side, factor in enumerate((k_factor, c_factor)):
        diag16 = factor[0, :, 0:256].astype(bf16)
        border16 = (factor[0, :, 256:512] * flag).astype(bf16)
        h_out[side] = dot(diag16.astype(f32).T, v_out[side]) + dot(border16.astype(f32).T, u_out[side])

    for t in range(1, 4):
        there = (d, lax.rem(x + t, NX) * NZ + z)
        behind = lax.rem(x + NX - t, NX)
        send(lead_b.at[x], lead_b.at[x], xb_s.at[t], xb_r.at[t], there).wait_send()
        send(lead_g.at[x], lead_g.at[x], xg_s.at[t], xg_r.at[t], there).wait_send()
        arrived(lead_b.at[behind], xb_r.at[t])
        arrived(lead_g.at[behind], xg_r.at[t])

    @pl.loop(1, 32)
    def _(t):
        send(tr.at[f], tr.at[f], tr_s.at[t], tr_r.at[t], (d, lax.rem(f + t, 32))).wait_send()
        arrived(tr.at[lax.rem(f + 32 - t, 32)], tr_r.at[t])

    sums_all = tr[0]
    for i in range(1, 32):
        sums_all = sums_all + tr[i]
    trace = [sums_all[i : i + 1, 0:1] for i in range(4)]
    total_tokens = counts[0]
    for i in range(1, 8):
        total_tokens = total_tokens + counts[i]
    inverse = 1.0 / jnp.full((1, 1), total_tokens.astype(f32), f32)
    width = 8192.0
    identity = jnp.where(rows == cols, 1.0, 0.0)

    def advance(side):
        factor, moment = (k_factor, c_factor)[side], (k_moment, c_moment)[side]
        f_new, m_new, half16 = (k_new, c_new)[side], (km_new, cm_new)[side], (k_half, c_half)[side]
        other_h = trace[2 - 2 * side] * inverse * inverse
        other_g = trace[3 - 2 * side] * damping
        diag = factor[0, :, 0:256]
        border = factor[0, :, 256:512] * flag
        lead = lead_b[...].reshape(512, 256)[side * 256 : side * 256 + 256, :].astype(f32)
        fresh = (other_h * h_out[side] + other_g * gram_out[side] - width * identity) / (2.0 * width)
        cross = dot(lead.T, other_h * u_out[side] + other_g * border) * flag / (2.0 * width)
        m_diag = momentum_rate * moment[0, :, 0:256] + fresh
        m_side = (momentum_rate * moment[0, :, 256:512] + cross) * flag
        n_diag = diag - step_rate * dot(diag, m_diag)
        n_side = (border - step_rate * (dot(lead, m_side) + dot(border, m_diag))) * flag
        f_new[0, :, 0:256] = n_diag
        f_new[0, :, 256:512] = n_side
        m_new[0, :, 0:256] = m_diag
        m_new[0, :, 256:512] = m_side
        half16[0:256, :] = n_diag.astype(bf16)
        half16[256:512, :] = n_side.astype(bf16)

    holder = lax.div(z, 4) == c
    root = jnp.logical_and(holder, x == y)
    j = lax.rem(z, 4)

    def quarter(t):
        return c_half.at[pl.ds(pl.multiple_of(t * 128, 128), 128)]

    def scatter_copy(t):
        to = lax.rem(x + t, NX)
        return send(quarter(to), cb.at[to, j], ca_s.at[t], ca_r, (d, to * NZ + z))

    advance(1)

    @pl.when(root)
    def _():
        for t in range(1, 4):
            scatter_copy(t).start()
        pltpu.make_async_copy(quarter(x), cb.at[x, j], ca_r).start()

    advance(0)
    k_diag, k_side = k_half[0:256, :], k_half[256:512, :]
    first = (dot16(grad[...], k_diag) + dot16(lead_g[...].reshape(1024, 256), k_side)).astype(bf16)
    lead_src[...] = dot16(first, k_side.T).astype(bf16).reshape(32, 32, 256)

    def border_x(t):
        to = lax.rem(x + t, NX)
        src = lead_src.at[pl.ds(pl.multiple_of(to * 8, 8), 8)]
        return send(src, lead_in.at[t], bo_s.at[t], bo_r.at[t], (d, to * NZ + z))

    def border_z(t):
        to = lax.rem(z + t, NZ)
        return send(lead_x.at[to], lead_z.at[t], bz_s.at[t], bz_r.at[t], (d, x * NZ + to))

    for t in (1, 3, 2):
        border_x(t).start()

    own[...] = dot16(first, k_diag.T)

    def ring_copy(t):
        return send(cb.at[x, j], cb.at[x, j], cz_s.at[t], cz_r.at[j], (d, x * NZ + lax.rem(z + t, NZ)))

    @pl.when(holder)
    def _():
        arrived(cb.at[x, j], ca_r)
        for t in range(1, 8):
            ring_copy(t).start()

    border = lead_src[pl.ds(pl.multiple_of(x * 8, 8), 8)].astype(f32)
    for t in (1, 3, 2):
        arrived(lead_in.at[t], bo_r.at[t])
        border = border + lead_in[t].astype(f32)
    lead_x[...] = border.astype(bf16)
    for t in range(1, 8):
        border_z(t).start()
    second[...] = own[...].astype(bf16)

    for i in range(4):

        @pl.when(jnp.logical_or(jnp.logical_not(holder), j != i))
        def _():
            arrived(cb.at[x, i], cz_r.at[i])

    def spread_copy(t, low):
        at = cb.at[x, 2 * low : 2 * low + 2]
        return send(at, at, cx_s.at[low, t], cx_r.at[low, t], (d, lax.rem(x + t, NX) * NZ + z))

    for t in (1, 3):
        spread_copy(t, 0).start()

    total = lead_x[z].astype(f32)
    for t in range(1, 8):
        arrived(lead_z.at[t], bz_r.at[t])
        total = total + lead_z[t].astype(f32)
    lead_sum[...] = total.astype(bf16)

    @pl.when(f > 0)
    def _():
        send(lead_sum, all_lead.at[f], ga_s, ga_r.at[f], (d, 0)).start()

    for t, low in ((1, 1), (3, 1), (2, 0), (2, 1)):
        spread_copy(t, low).start()

    @pl.when(f == 0)
    def _():
        all_lead[0] = lead_sum[...]
        for i in range(1, 32):
            arrived(all_lead.at[i], ga_r.at[i])
        second[...] = (own[...] + all_lead[...].reshape(1024, 256).astype(f32)).astype(bf16)

    src = second.at[0:256]

    @pl.when(d == 0)
    def _():
        for t in range(1, 8):
            send(src, lead_rows, ro_s.at[t], ro_r, (t, f)).start()
        pltpu.make_async_copy(src, lead_rows, ro_r).start()

    for t in range(1, 4):
        for low in range(2):
            arrived(cb.at[lax.rem(x + NX - t, NX), 2 * low : 2 * low + 2], cx_r.at[low, t])
    for i in range(4):
        diag = cb[0:2, i].reshape(256, 256)
        part[i] = dot16(diag.T, second[i * 256 : i * 256 + 256, :])
    arrived(lead_rows, ro_r)
    sum_term = jnp.zeros((256, 256), f32)
    for i in range(4):
        diag = cb[0:2, i].reshape(256, 256)
        side = cb[2:4, i].reshape(256, 256)
        third = (part[i] + dot16(side.T, lead_rows[...])).astype(bf16)
        own[i * 256 : i * 256 + 256, :] = dot16(diag, third)
        sum_term = sum_term + dot16(side, third)
    term[...] = sum_term.astype(bf16)

    @pl.when(d > 0)
    def _():
        send(term, terms.at[d], te_s, te_r.at[d], (0, f)).start()

    out[256:1024, :] = own[256:1024, :].astype(bf16)

    @pl.when(d > 0)
    def _():
        out[0:256, :] = own[0:256, :].astype(bf16)
        send(term, terms.at[d], te_s, te_r.at[d], (0, f)).wait_send()

    @pl.when(d == 0)
    def _():
        whole = own[0:256, :] + sum_term
        for t in range(1, 8):
            arrived(terms.at[t], te_r.at[t])
            whole = whole + terms[t].astype(f32)
        out[0:256, :] = whole.astype(bf16)
        for t in range(1, 8):
            send(src, lead_rows, ro_s.at[t], ro_r, (t, f)).wait_send()

    @pl.when(root)
    def _():
        for t in range(1, 4):
            scatter_copy(t).wait_send()

    @pl.when(holder)
    def _():
        for t in range(1, 8):
            ring_copy(t).wait_send()

    for t in range(1, 4):
        spread_copy(t, 0).wait_send()
        spread_copy(t, 1).wait_send()
        border_x(t).wait_send()
    for t in range(1, 8):
        border_z(t).wait_send()

    @pl.when(f > 0)
    def _():
        send(lead_sum, all_lead.at[f], ga_s, ga_r.at[f], (d, 0)).wait_send()
    for on in passed:
        on.wait_send()
    for side in range(2):
        half_copy(side).wait_send()
        quarter_copy(side).wait_send()
        for g in range(1, 4):
            z_copy(side, g).wait_send()
    for copies in tokens:
        for i, at, one, two in copies:
            if i > 0:
                one.wait_send()
                two.wait_send()

    @pl.when(f == 0)
    def _():
        @pl.loop(1, 32)
        def _(t):
            send(grad_piece(t), piece_g, s3.at[t], r3.at[0], (d, t)).wait_send()
            send(lead_piece(t), piece_b, s4.at[t], r3.at[1], (d, t)).wait_send()

    for side in range(2):

        @pl.when(mine == 0)
        def _():
            @pl.loop(0, 32)
            def _(t):
                @pl.when(jnp.logical_not(is_me(lead_target(t))))
                def _():
                    lead_send(side, t).wait_send()

        for m in range(2):

            @pl.when(jnp.logical_not(is_me((to_d, mine + 16 * m))))
            def _():
                rows_send(side, m).wait_send()

        for i in range(2):
            for t in range(4):
                share_send(side, i, t).wait_send()
            for t in range(1, 4):
                pass_send(side, i, t).wait_send()


def finish_body(*refs):
    for src, dst in zip(refs[:5], refs[5:]):
        dst[...] = src[...]


def per_device(acts, out_grads, token_counts, k_factor, c_factor, k_moment, c_moment, grad_weight):
    SM = pl.BlockSpec(memory_space=pltpu.SMEM)
    V = pltpu.VMEM
    results = [((1, 256, 512), f32)] * 4 + [((1024, 256), bf16)]
    held = call(
        step_body, "step",
        (token_counts, acts, out_grads, k_factor, c_factor, k_moment, c_moment, grad_weight),
        [SM, ANY, ANY] + [VM] * 5, results, [VM] * 5,
        [V((2, 256, 256), f32), V((2, 256, 256), f32), V((2, 256, 256), f32), V((2, 256, 256), f32),
         V((32, 32, 256), bf16), V((4, 8, 32, 256), bf16), V((8, 32, 256), bf16), V((8, 32, 256), bf16),
         V((1024, 256), f32), V((32, 256), bf16),
         V((32, 32, 256), bf16), V((1024, 256), bf16), V((256, 256), bf16), V((4, 4, 128, 256), bf16),
         V((256, 256), bf16), V((8, 256, 256), bf16), V((4, 256, 256), f32), V((512, 256), bf16), V((512, 256), bf16),
         V((2, 128, 8192), bf16), V((2, 16, 2, 64, 512), bf16), V((2, 2, 2, 64, 128), bf16),
         V((2, 32, 64, 512), bf16), V((2, 32, 64, 256), bf16), V((512, 256), bf16), V((16, 256), bf16),
         V((32, 256), bf16), V((2, 16, 4, 16, 256), bf16), V((2, 8, 4, 16, 256), bf16), V((2, 8, 4, 16, 256), bf16),
         V((2, 4, 4, 16, 256), bf16), V((2, 4, 4, 16, 256), bf16), V((2, 4, 4, 16, 256), bf16), V((2, 2, 2, 16, 256), bf16),
         V((2, 16, 3, 16, 256), bf16), V((32, 8, 128), f32), V((4, 8, 16, 256), bf16), V((4, 8, 32, 256), bf16),
         DMA((2,))] + [DMA((2, 32))] * 6 + [DMA((32,)), DMA((32,)), DMA((2,)),
         DMA((2, 16)), DMA((2, 16)), DMA((2, 2)), DMA((2, 16)), DMA((2, 32)), DMA((2, 16)), DMA((2, 2, 4)),
         DMA((2, 2, 4)), DMA((8,)), DMA((8,)), DMA((8,)), DMA((8,)), DMA((4,)), DMA((4,)), DMA((4,)), DMA((4,)),
         DMA((32,)), DMA((32,)),
         DMA((4,)), DMA((4,)), DMA((8,)), DMA((8,)), DMA, DMA((32,)), DMA((4,)), DMA, DMA((8,)), DMA((4,)), DMA((2, 4)), DMA((2, 4)),
         DMA((8,)), DMA, DMA, DMA((8,))],
        0,
    )
    return tuple(call(finish_body, "finish", held, [VM] * 5, results, [VM] * 5))


def solution(mesh):
    in_specs = (
        P(("dp", "fsdp"), None),
        P(("dp", "fsdp"), None),
        P(),
        P("fsdp", None, None),
        P("fsdp", None, None),
        P("fsdp", None, None),
        P("fsdp", None, None),
        P("dp", "fsdp"),
    )
    out_specs = (
        P("fsdp", None, None),
        P("fsdp", None, None),
        P("fsdp", None, None),
        P("fsdp", None, None),
        P("dp", "fsdp"),
    )
    return jax.shard_map(per_device, mesh=mesh, in_specs=in_specs, out_specs=out_specs, check_vma=False)
```

```python
import functools

import jax
import jax.numpy as jnp
from jax import lax
from jax.experimental import pallas as pl
from jax.experimental.pallas import tpu as pltpu
from jax.sharding import PartitionSpec as P

MESH = pl.DeviceIdType.MESH
highest = lax.Precision.HIGHEST
f32 = jnp.float32
bf16 = jnp.bfloat16

damping = 0.1
momentum_rate = 0.5
step_rate = 0.2

NX, NY, NZ = 4, 4, 8


def position():
    d = lax.axis_index("dp")
    f = lax.axis_index("fsdp")
    return lax.div(f, NZ), lax.div(d, 2), lax.rem(f, NZ), lax.rem(d, 2)


def device(x, y, z, c):
    return (y * 2 + c, x * NZ + z)


def class_of(x, y, z, c):
    return lax.rem(x, 2) * 8 + lax.rem(y, 2) * 4 + c * 2 + lax.rem(z, 2)


def send(src, dst, send_sem, recv_sem, target):
    return pltpu.make_async_remote_copy(
        src_ref=src, dst_ref=dst, send_sem=send_sem, recv_sem=recv_sem, device_id=target, device_id_type=MESH
    )


def arrived(dst, sem):
    pltpu.make_async_copy(dst, dst, sem).wait()


def greet(barrier, target):
    pl.semaphore_signal(barrier, inc=1, device_id=target, device_id_type=MESH)


ANY = pl.BlockSpec(memory_space=pl.ANY)
VM = pl.BlockSpec(memory_space=pltpu.VMEM)
DMA = pltpu.SemaphoreType.DMA


def call(body, name, ins, in_specs, outs, out_specs, scratch=(), cid=None):
    params = dict(collective_id=cid, has_side_effects=True) if cid is not None else {}
    return pl.pallas_call(
        body,
        out_shape=[jax.ShapeDtypeStruct(s, t) for s, t in outs],
        in_specs=in_specs,
        out_specs=out_specs,
        scratch_shapes=list(scratch),
        compiler_params=pltpu.CompilerParams(**params),
        name=name,
    )(*ins)


def dot(a, b):
    return jnp.dot(a, b, precision=highest, preferred_element_type=f32)


def dot16(a, b):
    return jnp.dot(a, b, preferred_element_type=f32)


def dot(a, b):
    return jnp.dot(a, b, precision=highest, preferred_element_type=f32)


def dot16(a, b):
    return jnp.dot(a, b, preferred_element_type=f32)


def step_body(
    counts, acts, grads, k_factor, c_factor, k_moment, c_moment, grad, k_new, c_new, km_new, cm_new, out,
    held, held_s, h_out, u_out, v_out, gram_out, lead_src, lead_in, lead_x, lead_z, own, lead_sum, all_lead, second, lead_rows, cb, term, terms, part, k_half,
    c_half, raw, xs, ls, xc, x0, b0, piece_b, piece_g, ps, py_in, qx, px_in, qz, pz_in, sm, st, tr, lead_b, lead_g,
    in_s, s1, r1, s2, r2, s5, r4, s3, s4, r3,
    rs_s, rs_r, de_s, de_r, a0_s, a0_r, ag_s, fw_s, zb_s, zb_r, zg_s, zg_r, xb_s, xb_r, xg_s, xg_r, tr_s, tr_r,
    bo_s, bo_r, bz_s, bz_r, ga_s, ga_r, ca_s, ca_r, cz_s, cz_r, cx_s, cx_r, ro_s, ro_r, te_s, te_r,
):
    x, y, z, c = position()
    d, f = lax.axis_index("dp"), lax.axis_index("fsdp")
    barrier = pltpu.get_barrier_semaphore()
    loads = [pltpu.make_async_copy(ref, raw.at[i], in_s.at[i]) for i, ref in enumerate((acts, grads))]
    for one in loads:
        one.start()
    partner = device(x, y, z, 1 - c)

    def cell(sign, a, b, g, e):
        return (
            lax.rem(x + sign * a + NX, NX),
            lax.rem(y + sign * b + NY, NY),
            lax.rem(z + sign * g + NZ, NZ),
            lax.rem(c + e, 2),
        )

    offsets = [(a, b, g, e) for a in (0, 1) for b in (0, 1) for g in (0, 1) for e in (0, 1)]
    mine = class_of(x, y, z, c)
    xi, yi, zi = lax.div(x, 2), lax.div(y, 2), lax.div(z, 2)
    slot = (yi * 8 + xi * 4 + zi, xi * 8 + yi * 4 + zi)
    mate_y = device(x, lax.rem(y + 2, NY), z, c)
    mate_x = device(lax.rem(x + 2, NX), y, z, c)

    def mate_z(g):
        return device(x, y, lax.rem(z + 2 * g, NZ), c)

    k = lax.rem(f, 16)
    px, py, pc, pz = lax.div(k, 8), lax.rem(lax.div(k, 4), 2), lax.rem(lax.div(k, 2), 2), lax.rem(k, 2)

    def group_for(parity):
        return lax.rem(2 * yi + parity + lax.rem(zi, 2), NY) * 2 + lax.div(zi, 2)

    def slots_at(there_y, side):
        shift = lax.rem(there_y + py, 2)
        half_y = lax.div(lax.rem(there_y - shift + NY, NY), 2)
        low = half_y * (8, 4)[side] + 2 * c + shift
        return [low, low + (4, 8)[side]]

    def owner(j, qx, qy, qz, qc):
        return device(qx + 2 * lax.rem(lax.div(j, 4), 2), qy + 2 * lax.div(j, 8), qz + 2 * lax.rem(j, 4), qc)

    to_d = group_for(lax.rem(y, 2))
    from_j = [slots_at(y, side) for side in range(2)]

    def is_me(there):
        return jnp.logical_and(there[0] == d, there[1] == f)

    def lead_target(t):
        return (group_for(lax.rem(lax.div(t, 4), 2)), t)

    for sign in (1, -1):
        for o in offsets:
            if o[:3] == (0, 0, 0) and (o[3] == 0 or sign == -1):
                continue
            greet(barrier, device(*cell(sign, *o)))
    for there in (mate_y, mate_x, mate_z(1), mate_z(2), mate_z(3)):
        greet(barrier, there)

    @pl.loop(1, 32)
    def _(t):
        greet(barrier, (d, lax.rem(f + t, 32)))

    for t in range(1, 4):
        greet(barrier, device(x, lax.rem(y + t, NY), z, c))
    for j in from_j[0]:
        for there in (owner(j, px, py, pz, pc), owner(j, 0, 0, 0, 0)):

            @pl.when(jnp.logical_not(is_me(there)))
            def _():
                greet(barrier, there)

    @pl.when(d == 0)
    def _():
        for t in range(1, 8):
            greet(barrier, (t, f))

    @pl.when(d > 0)
    def _():
        greet(barrier, (0, f))

    limit = counts[0] * jnp.where(d == 0, 1, 0)
    for i in range(1, 8):
        limit = limit + counts[i] * jnp.where(d == i, 1, 0)
    kept = []
    for h in range(2):
        at_slot = lax.broadcasted_iota(jnp.int32, (64, 256), 0) + (f * 128 + h * 64)
        kept.append(jnp.where(at_slot < limit, 1.0, 0.0).astype(bf16))

    def mask(side):
        loads[side].wait()
        for h in range(2):
            rows = slice(h * 64, h * 64 + 64)
            lead = raw[side, rows, 0:256] * kept[h]
            ls[side, 0, h, :, :] = lead[:, 0:128]
            ls[side, 1, h, :, :] = lead[:, 128:256]
            for i in range(16):
                for m in range(2):
                    n = m * 16 + i
                    cols = slice(m * 256, m * 256 + 256)
                    xs[side, i, h, :, cols] = raw[side, rows, n * 256 : n * 256 + 256] * kept[h]

    half = pl.ds(pl.multiple_of(c * 128, 128), 128)
    other_half = pl.ds(pl.multiple_of(128 - c * 128, 128), 128)

    def exchange(side):
        copies = []
        for i in (14, 15, 12, 13, 10, 11, 6, 7, 8, 9, 4, 5, 2, 3, 1, 0):
            for h, sign in ((0, 1), (1, -1)):
                there = cell(sign, *offsets[i])
                to = class_of(*there)
                at = h * 16 + i
                if i == 0:
                    one = pltpu.make_async_copy(xs.at[side, to, h], xc.at[side, at], r1.at[side, at])
                    two = pltpu.make_async_copy(ls.at[side, c, h], x0.at[side, at, :, half], r2.at[side, at])
                else:
                    tc = there[3]
                    to_half = pl.ds(pl.multiple_of(tc * 128, 128), 128)
                    dst = device(*there)
                    one = send(xs.at[side, to, h], xc.at[side, at], s1.at[side, at], r1.at[side, at], dst)
                    two = send(ls.at[side, tc, h], x0.at[side, at, :, to_half], s2.at[side, at], r2.at[side, at], dst)
                two.start()
                one.start()
                copies.append((i, at, one, two))
        return copies

    def collect(side, copies):
        passed = []
        for i, at, one, two in copies:
            got = x0.at[side, at, :, half]
            arrived(got, r2.at[side, at])
            on = send(got, x0.at[side, at ^ 1, :, half], s5.at[side, at], r4.at[side, at ^ 1], partner)
            on.start()
            passed.append(on)
        for i, at, one, two in copies:
            arrived(xc.at[side, at], r1.at[side, at])
        for i, at, one, two in copies:
            arrived(x0.at[side, at, :, other_half], r4.at[side, at])
        return passed

    def grad_piece(t):
        return grad.at[pl.ds(pl.multiple_of(t * 32, 32), 32)]

    def lead_piece(t):
        return b0.at[pl.ds(pl.multiple_of(t * 16, 16), 16)]

    @pl.when(f == 0)
    def _():
        b0[0:256, :] = k_factor[0, :, 0:256].astype(bf16)
        b0[256:512, :] = c_factor[0, :, 0:256].astype(bf16)

    mask(0)
    to_self = jnp.where(is_me((to_d, mine)), 1, 0) + jnp.where(is_me((to_d, mine + 16)), 1, 0)
    lead_self = jnp.where(is_me(lead_target(f)), 1, 0)
    pl.semaphore_wait(
        barrier, 29 + 5 + 31 + 3 + 2 - to_self + jnp.where(mine == 0, 32 - lead_self, 0) + jnp.where(d == 0, 7, 1)
    )
    tokens = [exchange(0)]
    mask(1)
    tokens.append(exchange(1))

    @pl.when(f == 0)
    def _():
        pltpu.make_async_copy(grad_piece(0), piece_g, r3.at[0]).start()
        pltpu.make_async_copy(lead_piece(0), piece_b, r3.at[1]).start()

        @pl.loop(1, 32)
        def _(t):
            send(grad_piece(t), piece_g, s3.at[t], r3.at[0], (d, t)).start()
            send(lead_piece(t), piece_b, s4.at[t], r3.at[1], (d, t)).start()


    flag = jnp.where(f > 0, 1.0, 0.0)
    for side, factor in enumerate((k_factor, c_factor)):
        diag = factor[0, :, 0:256]
        border = factor[0, :, 256:512] * flag
        gram_out[side] = dot(diag.T, diag) + dot(border.T, border)
        tr_g = jnp.sum(diag * diag) + jnp.sum(border * border)
        tr[f, side * 2 + 1 : side * 2 + 2, :] = jnp.full((1, 128), tr_g, f32)
    tr[f, 4:8, :] = jnp.zeros((4, 128), f32)

    dims = (((0,), (0,)), ((), ()))

    def gram(side):
        lead = x0[side].reshape(2048, 256)
        a = xc[side, :, :, 0:256].reshape(2048, 256)
        b = xc[side, :, :, 256:512].reshape(2048, 256)
        for i, (left, right) in enumerate(((a, a), (b, b), (lead, a), (lead, b))):
            g = lax.dot_general(left, right, dims, preferred_element_type=f32)
            ps[side, :, i, :, :] = g.astype(bf16).reshape(16, 16, 256)

    bits = ((yi, xi), (xi, yi))
    halves = ((mate_y, mate_x), (mate_x, mate_y))

    def half_copy(side):
        src = ps.at[side, pl.ds((1 - bits[side][0]) * 8, 8)]
        return send(src, py_in.at[side], rs_s.at[side, 0], rs_r.at[side, 0], halves[side][0])

    def quarter_copy(side):
        src = qx.at[side, pl.ds((1 - bits[side][1]) * 4, 4)]
        return send(src, px_in.at[side], rs_s.at[side, 1], rs_r.at[side, 1], halves[side][1])

    def z_copy(side, g):
        src = qz.at[side, lax.rem(zi + g, 4)]
        return send(src, pz_in.at[side, g], rs_s.at[side, 1 + g], rs_r.at[side, 1 + g], mate_z(g))

    def over_half(side):
        arrived(py_in.at[side], rs_r.at[side, 0])
        qx[side] = (ps[side, pl.ds(bits[side][0] * 8, 8)].astype(f32) + py_in[side].astype(f32)).astype(bf16)
        quarter_copy(side).start()

    def over_quarter(side):
        arrived(px_in.at[side], rs_r.at[side, 1])
        qz[side] = (qx[side, pl.ds(bits[side][1] * 4, 4)].astype(f32) + px_in[side].astype(f32)).astype(bf16)
        for g in range(1, 4):
            z_copy(side, g).start()

    passed = collect(0, tokens[0])
    gram(0)
    half_copy(0).start()
    passed += collect(1, tokens[1])
    gram(1)
    half_copy(1).start()
    def total(side):
        value = qz[side, zi].astype(f32)
        for g in range(1, 4):
            arrived(pz_in.at[side, g], rs_r.at[side, 1 + g])
            value = value + pz_in[side, g].astype(f32)
        value = value.astype(bf16)
        for m in range(2):
            for q in range(2):
                sm[side, m, q] = value[2 * q + m]

    def lead_send(side, t):
        return send(sm.at[side, 0, 0], st.at[side, slot[side], 2], a0_s.at[side, t], a0_r.at[side, slot[side]], lead_target(t))

    def rows_send(side, m):
        there = (to_d, mine + 16 * m)
        return send(sm.at[side, m], st.at[side, slot[side], 0:2], de_s.at[side, m], de_r.at[side, slot[side]], there)

    def deliver(side):
        @pl.when(mine == 0)
        def _():
            @pl.loop(0, 32)
            def _(t):
                me = is_me(lead_target(t))

                @pl.when(me)
                def _():
                    pltpu.make_async_copy(sm.at[side, 0, 0], st.at[side, slot[side], 2], a0_r.at[side, slot[side]]).start()

                @pl.when(jnp.logical_not(me))
                def _():
                    lead_send(side, t).start()

        for m in range(2):
            me = is_me((to_d, mine + 16 * m))

            @pl.when(me)
            def _():
                pltpu.make_async_copy(sm.at[side, m], st.at[side, slot[side], 0:2], de_r.at[side, slot[side]]).start()

            @pl.when(jnp.logical_not(me))
            def _():
                rows_send(side, m).start()

    def share_send(side, i, t):
        there = device(x, lax.rem(y + t, NY), z, c) if t > 0 else partner
        at = st.at[side, from_j[side][i]]
        return send(at, at, ag_s.at[side, i, t], de_r.at[side, from_j[side][i]], there)

    def pass_send(side, i, t):
        j = slots_at(lax.rem(y + NY - t, NY), side)[i]
        return send(st.at[side, j], st.at[side, j], fw_s.at[side, i, t], de_r.at[side, j], partner)

    def share(side):
        for i in range(2):
            arrived(st.at[side, from_j[side][i], 0:2], de_r.at[side, from_j[side][i]])
            arrived(st.at[side, from_j[side][i], 2], a0_r.at[side, from_j[side][i]])
            for t in (1, 2, 3, 0):
                share_send(side, i, t).start()

    def pass_on(side):
        for t in (1, 3, 2):
            for i in range(2):
                j = slots_at(lax.rem(y + NY - t, NY), side)[i]
                arrived(st.at[side, j], de_r.at[side, j])
                pass_send(side, i, t).start()

    over_half(0)
    arrived(piece_g, r3.at[0])
    arrived(piece_b, r3.at[1])
    own_b = pltpu.make_async_copy(piece_b, lead_b.at[x, z], zb_r.at[0])
    own_g = pltpu.make_async_copy(piece_g, lead_g.at[x, z], zg_r.at[0])
    own_b.start()
    own_g.start()
    for t in range(1, 8):
        there = (d, x * NZ + lax.rem(z + t, NZ))
        send(piece_b, lead_b.at[x, z], zb_s.at[t], zb_r.at[t], there).start()
        send(piece_g, lead_g.at[x, z], zg_s.at[t], zg_r.at[t], there).start()
    over_half(1)
    over_quarter(0)
    over_quarter(1)
    total(0)
    deliver(0)
    total(1)
    deliver(1)
    own_b.wait()
    own_g.wait()
    for t in range(1, 8):
        there = (d, x * NZ + lax.rem(z + t, NZ))
        behind = lax.rem(z + NZ - t, NZ)
        send(piece_b, lead_b.at[x, z], zb_s.at[t], zb_r.at[t], there).wait_send()
        send(piece_g, lead_g.at[x, z], zg_s.at[t], zg_r.at[t], there).wait_send()
        arrived(lead_b.at[x, behind], zb_r.at[t])
        arrived(lead_g.at[x, behind], zg_r.at[t])
    for t in range(1, 4):
        there = (d, lax.rem(x + t, NX) * NZ + z)
        send(lead_b.at[x], lead_b.at[x], xb_s.at[t], xb_r.at[t], there).start()
        send(lead_g.at[x], lead_g.at[x], xg_s.at[t], xg_r.at[t], there).start()
    share(0)
    share(1)
    pass_on(0)
    pass_on(1)

    rows = lax.broadcasted_iota(jnp.int32, (256, 256), 0)
    cols = lax.broadcasted_iota(jnp.int32, (256, 256), 1)

    def second_moment(side):
        for j in range(16):
            @pl.when(lax.div(j % 4, 2) != c)
            def _():
                arrived(st.at[side, j], de_r.at[side, j])

        factor = (k_factor, c_factor)[side]
        diag16 = factor[0, :, 0:256].astype(bf16)
        border16 = (factor[0, :, 256:512] * flag).astype(bf16)
        a = st[side, :, 0].reshape(256, 256)
        cross = st[side, :, 1].reshape(256, 256)
        lead = st[side, :, 2].reshape(256, 256)
        u = dot16(cross, diag16) + dot16(lead, border16)
        v = dot16(a, diag16) + dot16(cross.T, border16)
        tr_h = jnp.sum(diag16.astype(f32) * v) + jnp.sum(border16.astype(f32) * u)
        tr[f, side * 2 : side * 2 + 1, :] = jnp.full((1, 128), tr_h, f32)
        u_out[side] = u
        v_out[side] = v

    second_moment(0)
    second_moment(1)

    @pl.loop(1, 32)
    def _(t):
        send(tr.at[f], tr.at[f], tr_s.at[t], tr_r.at[t], (d, lax.rem(f + t, 32))).start()

    for side, factor in enumerate((k_factor, c_factor)):
        diag16 = factor[0, :, 0:256].astype(bf16)
        border16 = (factor[0, :, 256:512] * flag).astype(bf16)
        h_out[side] = dot(diag16.astype(f32).T, v_out[side]) + dot(border16.astype(f32).T, u_out[side])

    for t in range(1, 4):
        there = (d, lax.rem(x + t, NX) * NZ + z)
        behind = lax.rem(x + NX - t, NX)
        send(lead_b.at[x], lead_b.at[x], xb_s.at[t], xb_r.at[t], there).wait_send()
        send(lead_g.at[x], lead_g.at[x], xg_s.at[t], xg_r.at[t], there).wait_send()
        arrived(lead_b.at[behind], xb_r.at[t])
        arrived(lead_g.at[behind], xg_r.at[t])

    @pl.loop(1, 32)
    def _(t):
        send(tr.at[f], tr.at[f], tr_s.at[t], tr_r.at[t], (d, lax.rem(f + t, 32))).wait_send()
        arrived(tr.at[lax.rem(f + 32 - t, 32)], tr_r.at[t])

    sums_all = tr[0]
    for i in range(1, 32):
        sums_all = sums_all + tr[i]
    trace = [sums_all[i : i + 1, 0:1] for i in range(4)]
    total_tokens = counts[0]
    for i in range(1, 8):
        total_tokens = total_tokens + counts[i]
    inverse = 1.0 / jnp.full((1, 1), total_tokens.astype(f32), f32)
    width = 8192.0
    identity = jnp.where(rows == cols, 1.0, 0.0)

    def advance(side):
        factor, moment = (k_factor, c_factor)[side], (k_moment, c_moment)[side]
        half16 = (k_half, c_half)[side]
        other_h = trace[2 - 2 * side] * inverse * inverse
        other_g = trace[3 - 2 * side] * damping
        diag = factor[0, :, 0:256]
        border = factor[0, :, 256:512] * flag
        lead = lead_b[...].reshape(512, 256)[side * 256 : side * 256 + 256, :].astype(f32)
        fresh = (other_h * h_out[side] + other_g * gram_out[side] - width * identity) / (2.0 * width)
        cross = dot(lead.T, other_h * u_out[side] + other_g * border) * flag / (2.0 * width)
        m_diag = momentum_rate * moment[0, :, 0:256] + fresh
        m_side = (momentum_rate * moment[0, :, 256:512] + cross) * flag
        n_diag = diag - step_rate * dot(diag, m_diag)
        n_side = (border - step_rate * (dot(lead, m_side) + dot(border, m_diag))) * flag
        held[side, :, 0:256] = n_diag
        held[side, :, 256:512] = n_side
        held[2 + side, :, 0:256] = m_diag
        held[2 + side, :, 256:512] = m_side
        half16[0:256, :] = n_diag.astype(bf16)
        half16[256:512, :] = n_side.astype(bf16)

    holder = lax.div(z, 4) == c
    root = jnp.logical_and(holder, x == y)
    j = lax.rem(z, 4)

    def quarter(t):
        return c_half.at[pl.ds(pl.multiple_of(t * 128, 128), 128)]

    def scatter_copy(t):
        to = lax.rem(x + t, NX)
        return send(quarter(to), cb.at[to, j], ca_s.at[t], ca_r, (d, to * NZ + z))

    advance(1)

    @pl.when(root)
    def _():
        for t in range(1, 4):
            scatter_copy(t).start()
        pltpu.make_async_copy(quarter(x), cb.at[x, j], ca_r).start()

    advance(0)
    stores = [
        pltpu.make_async_copy(held.at[i], ref.at[0], held_s.at[i]) for i, ref in enumerate((k_new, c_new, km_new, cm_new))
    ]
    k_diag, k_side = k_half[0:256, :], k_half[256:512, :]
    first = (dot16(grad[...], k_diag) + dot16(lead_g[...].reshape(1024, 256), k_side)).astype(bf16)
    lead_src[...] = dot16(first, k_side.T).astype(bf16).reshape(32, 32, 256)

    def border_x(t):
        to = lax.rem(x + t, NX)
        src = lead_src.at[pl.ds(pl.multiple_of(to * 8, 8), 8)]
        return send(src, lead_in.at[t], bo_s.at[t], bo_r.at[t], (d, to * NZ + z))

    def border_z(t):
        to = lax.rem(z + t, NZ)
        return send(lead_x.at[to], lead_z.at[t], bz_s.at[t], bz_r.at[t], (d, x * NZ + to))

    for t in (1, 3, 2):
        border_x(t).start()
    for store in stores:
        store.start()

    own[...] = dot16(first, k_diag.T)

    def ring_copy(t):
        return send(cb.at[x, j], cb.at[x, j], cz_s.at[t], cz_r.at[j], (d, x * NZ + lax.rem(z + t, NZ)))

    @pl.when(holder)
    def _():
        arrived(cb.at[x, j], ca_r)
        for t in range(1, 8):
            ring_copy(t).start()

    border = lead_src[pl.ds(pl.multiple_of(x * 8, 8), 8)].astype(f32)
    for t in (1, 3, 2):
        arrived(lead_in.at[t], bo_r.at[t])
        border = border + lead_in[t].astype(f32)
    lead_x[...] = border.astype(bf16)
    for t in range(1, 8):
        border_z(t).start()
    second[...] = own[...].astype(bf16)

    for i in range(4):

        @pl.when(jnp.logical_or(jnp.logical_not(holder), j != i))
        def _():
            arrived(cb.at[x, i], cz_r.at[i])

    def spread_copy(t, low):
        at = cb.at[x, 2 * low : 2 * low + 2]
        return send(at, at, cx_s.at[low, t], cx_r.at[low, t], (d, lax.rem(x + t, NX) * NZ + z))

    for t in (1, 3):
        spread_copy(t, 0).start()

    total = lead_x[z].astype(f32)
    for t in range(1, 8):
        arrived(lead_z.at[t], bz_r.at[t])
        total = total + lead_z[t].astype(f32)
    lead_sum[...] = total.astype(bf16)

    @pl.when(f > 0)
    def _():
        send(lead_sum, all_lead.at[f], ga_s, ga_r.at[f], (d, 0)).start()

    def came(t, low):
        return cb.at[lax.rem(x + NX - t, NX), 2 * low : 2 * low + 2]

    def relay_copy(t):
        low = t // 2
        at = came(t, low)
        return send(at, at, cx_s.at[low, 2], cx_r.at[low, 2], (d, lax.rem(x + t, NX) * NZ + z))

    for t in (1, 3):
        spread_copy(t, 1).start()
    for t in (1, 3):
        arrived(came(t, t // 2), cx_r.at[t // 2, t])
        relay_copy(t).start()

    @pl.when(f == 0)
    def _():
        all_lead[0] = lead_sum[...]
        for i in range(1, 32):
            arrived(all_lead.at[i], ga_r.at[i])
        second[...] = (own[...] + all_lead[...].reshape(1024, 256).astype(f32)).astype(bf16)

    src = second.at[0:256]

    @pl.when(d == 0)
    def _():
        for t in range(1, 8):
            send(src, lead_rows, ro_s.at[t], ro_r, (t, f)).start()
        pltpu.make_async_copy(src, lead_rows, ro_r).start()

    for t, low in ((1, 1), (3, 0), (2, 0), (2, 1)):
        arrived(came(t, low), cx_r.at[low, t])
    for i in range(4):
        diag = cb[0:2, i].reshape(256, 256)
        part[i] = dot16(diag.T, second[i * 256 : i * 256 + 256, :])
    arrived(lead_rows, ro_r)
    sum_term = jnp.zeros((256, 256), f32)
    for i in range(4):
        diag = cb[0:2, i].reshape(256, 256)
        side = cb[2:4, i].reshape(256, 256)
        third = (part[i] + dot16(side.T, lead_rows[...])).astype(bf16)
        own[i * 256 : i * 256 + 256, :] = dot16(diag, third)
        sum_term = sum_term + dot16(side, third)
    term[...] = sum_term.astype(bf16)

    @pl.when(d > 0)
    def _():
        send(term, terms.at[d], te_s, te_r.at[d], (0, f)).start()

    out[256:1024, :] = own[256:1024, :].astype(bf16)

    @pl.when(d > 0)
    def _():
        out[0:256, :] = own[0:256, :].astype(bf16)
        send(term, terms.at[d], te_s, te_r.at[d], (0, f)).wait_send()

    @pl.when(d == 0)
    def _():
        whole = own[0:256, :] + sum_term
        for t in range(1, 8):
            arrived(terms.at[t], te_r.at[t])
            whole = whole + terms[t].astype(f32)
        out[0:256, :] = whole.astype(bf16)
        for t in range(1, 8):
            send(src, lead_rows, ro_s.at[t], ro_r, (t, f)).wait_send()

    @pl.when(root)
    def _():
        for t in range(1, 4):
            scatter_copy(t).wait_send()

    @pl.when(holder)
    def _():
        for t in range(1, 8):
            ring_copy(t).wait_send()

    for t in (1, 3):
        spread_copy(t, 0).wait_send()
        spread_copy(t, 1).wait_send()
        relay_copy(t).wait_send()
    for t in range(1, 4):
        border_x(t).wait_send()
    for t in range(1, 8):
        border_z(t).wait_send()

    @pl.when(f > 0)
    def _():
        send(lead_sum, all_lead.at[f], ga_s, ga_r.at[f], (d, 0)).wait_send()
    for store in stores:
        store.wait()
    for on in passed:
        on.wait_send()
    for side in range(2):
        half_copy(side).wait_send()
        quarter_copy(side).wait_send()
        for g in range(1, 4):
            z_copy(side, g).wait_send()
    for copies in tokens:
        for i, at, one, two in copies:
            if i > 0:
                one.wait_send()
                two.wait_send()

    @pl.when(f == 0)
    def _():
        @pl.loop(1, 32)
        def _(t):
            send(grad_piece(t), piece_g, s3.at[t], r3.at[0], (d, t)).wait_send()
            send(lead_piece(t), piece_b, s4.at[t], r3.at[1], (d, t)).wait_send()

    for side in range(2):

        @pl.when(mine == 0)
        def _():
            @pl.loop(0, 32)
            def _(t):
                @pl.when(jnp.logical_not(is_me(lead_target(t))))
                def _():
                    lead_send(side, t).wait_send()

        for m in range(2):

            @pl.when(jnp.logical_not(is_me((to_d, mine + 16 * m))))
            def _():
                rows_send(side, m).wait_send()

        for i in range(2):
            for t in range(4):
                share_send(side, i, t).wait_send()
            for t in range(1, 4):
                pass_send(side, i, t).wait_send()


def finish_body(*refs):
    buffers, flat, sems = refs[10:]
    moves = []
    for i in range(5):
        src, dst = (refs[i].at[0], refs[5 + i].at[0]) if i < 4 else (refs[i], refs[5 + i])
        middle = buffers.at[i] if i < 4 else flat
        moves.append(
            (pltpu.make_async_copy(src, middle, sems.at[0, i]), pltpu.make_async_copy(middle, dst, sems.at[1, i]))
        )
    for load, _ in moves:
        load.start()
    for load, store in moves:
        load.wait()
        store.start()
    for _, store in moves:
        store.wait()


def per_device(acts, out_grads, token_counts, k_factor, c_factor, k_moment, c_moment, grad_weight):
    SM = pl.BlockSpec(memory_space=pltpu.SMEM)
    V = pltpu.VMEM
    results = [((1, 256, 512), f32)] * 4 + [((1024, 256), bf16)]
    held = call(
        step_body, "step",
        (token_counts, acts, out_grads, k_factor, c_factor, k_moment, c_moment, grad_weight),
        [SM, ANY, ANY] + [VM] * 5, results, [ANY] * 4 + [VM],
        [V((4, 256, 512), f32), DMA((4,)), V((2, 256, 256), f32), V((2, 256, 256), f32), V((2, 256, 256), f32), V((2, 256, 256), f32),
         V((32, 32, 256), bf16), V((4, 8, 32, 256), bf16), V((8, 32, 256), bf16), V((8, 32, 256), bf16),
         V((1024, 256), f32), V((32, 256), bf16),
         V((32, 32, 256), bf16), V((1024, 256), bf16), V((256, 256), bf16), V((4, 4, 128, 256), bf16),
         V((256, 256), bf16), V((8, 256, 256), bf16), V((4, 256, 256), f32), V((512, 256), bf16), V((512, 256), bf16),
         V((2, 128, 8192), bf16), V((2, 16, 2, 64, 512), bf16), V((2, 2, 2, 64, 128), bf16),
         V((2, 32, 64, 512), bf16), V((2, 32, 64, 256), bf16), V((512, 256), bf16), V((16, 256), bf16),
         V((32, 256), bf16), V((2, 16, 4, 16, 256), bf16), V((2, 8, 4, 16, 256), bf16), V((2, 8, 4, 16, 256), bf16),
         V((2, 4, 4, 16, 256), bf16), V((2, 4, 4, 16, 256), bf16), V((2, 4, 4, 16, 256), bf16), V((2, 2, 2, 16, 256), bf16),
         V((2, 16, 3, 16, 256), bf16), V((32, 8, 128), f32), V((4, 8, 16, 256), bf16), V((4, 8, 32, 256), bf16),
         DMA((2,))] + [DMA((2, 32))] * 6 + [DMA((32,)), DMA((32,)), DMA((2,)),
         DMA((2, 16)), DMA((2, 16)), DMA((2, 2)), DMA((2, 16)), DMA((2, 32)), DMA((2, 16)), DMA((2, 2, 4)),
         DMA((2, 2, 4)), DMA((8,)), DMA((8,)), DMA((8,)), DMA((8,)), DMA((4,)), DMA((4,)), DMA((4,)), DMA((4,)),
         DMA((32,)), DMA((32,)),
         DMA((4,)), DMA((4,)), DMA((8,)), DMA((8,)), DMA, DMA((32,)), DMA((4,)), DMA, DMA((8,)), DMA((4,)), DMA((2, 4)), DMA((2, 4)),
         DMA((8,)), DMA, DMA, DMA((8,))],
        0,
    )
    scratch = [V((4, 256, 512), f32), V((1024, 256), bf16), DMA((2, 5))]
    return tuple(call(finish_body, "finish", held, [ANY] * 5, results, [ANY] * 5, scratch))


def solution(mesh):
    in_specs = (
        P(("dp", "fsdp"), None),
        P(("dp", "fsdp"), None),
        P(),
        P("fsdp", None, None),
        P("fsdp", None, None),
        P("fsdp", None, None),
        P("fsdp", None, None),
        P("dp", "fsdp"),
    )
    out_specs = (
        P("fsdp", None, None),
        P("fsdp", None, None),
        P("fsdp", None, None),
        P("fsdp", None, None),
        P("dp", "fsdp"),
    )
    return jax.shard_map(per_device, mesh=mesh, in_specs=in_specs, out_specs=out_specs, check_vma=False)
```
